1024 devices in a mesh: ctx: 32 (over y, z_hi, core), tp: 8 (over x), dp: 4 (over z_lo).
Axes of the slice: x: 8, y: 8, z: 8 (z_hi: 2, z_lo: 4; z = z_hi * 4 + z_lo), core: 2. Of those that a mesh axis runs over, the one named last changes fastest.
Arguments:
- out_grad: bfloat16 [4, 4096, 4096], P('dp', ('ctx', 'tp')), may hold values from -6 to 6
- gate_in: bfloat16 [4, 4096, 4096], P('dp', 'tp', 'ctx'), may hold values from -6 to 6
- conv_in: bfloat16 [4, 4096, 4096], P('dp', 'tp', 'ctx'), may hold values from -6 to 6
- filter_raw: float32 [4096, 4096], P(('tp', 'ctx')), may hold values from -6 to 6
- out_weight: bfloat16 [4096, 4096], P('tp'), may hold values from -0.09375 to 0.09375
Outputs:
- gate_grad_out: bfloat16 [4, 4096, 4096], P('dp', 'tp', 'ctx')
- conv_grad_out: bfloat16 [4, 4096, 4096], P('dp', 'tp', 'ctx')
- filter_grad_out: float32 [4096, 4096], P(('tp', 'ctx', 'dp'))
The draws below stay inside these ranges and needn't reach their ends.
All inputs are finite; a program needn't handle non-finite values.
Results may differ from the reference program's by a relative error of at most 0.0049.
Values may be sent and summed in bfloat16 or wider, within the bound.
A program may use at most 32 MiB of HBM per device.

```python
import jax
import jax.numpy as jnp
from jax import lax

D = 4096
LEN = 4096
SEQS = 4


def steps_of(rng, shape, split, smallest, high):
    loudness = 1.0
    for axis_at, parts in split:
        heights = jax.random.uniform(jax.random.fold_in(jax.random.fold_in(rng, 6), axis_at), (parts,), jnp.float32, smallest / len(split), high / len(split))
        loudness = loudness * jnp.repeat(jnp.exp(heights), shape[axis_at] // parts).reshape((-1,) + (1,) * (len(shape) - 1 - axis_at))
    return loudness


def noise(stream_key, shape, spread, limit, split=(), kind=jnp.bfloat16):
    entries = spread * jax.random.normal(stream_key, shape, jnp.float32)
    if split:
        entries = entries * steps_of(stream_key, shape, split, -0.22, 0.18)
    return jnp.clip(entries, -limit, limit).astype(kind)


def setup_inputs(seed: int = 0) -> dict:
    splits = jax.random.split(jax.random.key(seed), 6)
    return {
        "out_grad": noise(splits[0], (SEQS, LEN, D), 1.0, 6.0, ((0, 4), (1, 256))),
        "gate_in": noise(splits[1], (SEQS, D, LEN), 1.0, 6.0, ((0, 4), (1, 8), (2, 32))),
        "conv_in": noise(splits[2], (SEQS, D, LEN), 1.0, 6.0, ((0, 4), (1, 8), (2, 32))),
        "filter_raw": noise(splits[3], (D, LEN), 1.0, 6.0, ((0, 256),), jnp.float32),
        "out_weight": noise(splits[4], (D, D), D ** -0.5, 0.09375, ((0, 8),)),
    }


def reference(out_grad, gate_in, conv_in, filter_raw, out_weight):
    total_len = 2 * LEN
    root_len = jnp.sqrt(jnp.float32(LEN))
    filt = filter_raw / root_len
    spec_filt = jnp.fft.rfft(filt, n=total_len, axis=-1)

    def one_seq(total, items):
        grad_seq, gate_seq, conv_seq = items
        unit_grad = jnp.dot(out_weight, jnp.transpose(grad_seq), preferred_element_type=jnp.float32)
        gate_grad = (unit_grad * gate_seq.astype(jnp.float32)).astype(jnp.bfloat16)
        spec_conv = jnp.fft.rfft(conv_seq.astype(jnp.float32), n=total_len, axis=-1)
        spec_gate = jnp.fft.rfft(gate_grad.astype(jnp.float32), n=total_len, axis=-1)
        conv_out = jnp.fft.irfft(spec_filt * spec_conv, n=total_len, axis=-1)[:, :LEN].astype(jnp.bfloat16)
        conv_grad = jnp.fft.irfft(jnp.conj(spec_filt) * spec_gate, n=total_len, axis=-1)[:, :LEN].astype(jnp.bfloat16)
        filt_term = jnp.fft.irfft(spec_gate * jnp.conj(spec_conv), n=total_len, axis=-1)[:, :LEN] / root_len
        gate_out = (unit_grad * conv_out.astype(jnp.float32)).astype(jnp.bfloat16)
        return (total + filt_term, (gate_out, conv_grad))
    total, (gate_grad_out, conv_grad_out) = lax.scan(one_seq, jnp.zeros((D, LEN), jnp.float32), (out_grad, gate_in, conv_in))
    return (gate_grad_out, conv_grad_out, total)
```

```python
import functools
import math

import jax
import jax.numpy as jnp
import numpy as np
from jax import lax
from jax.experimental import pallas as pl
from jax.experimental.pallas import tpu as pltpu
from jax.sharding import PartitionSpec as P

MESH = pl.DeviceIdType.MESH
LANES = 128
CHANS = 16
CHUNKS = 4


def wave(order, index):
    angle = 2.0 * math.pi * (index % order) / order
    return (math.cos(angle), math.sin(angle))


def plus(left, right):
    if left is None:
        return right
    if right is None:
        return left
    return left + right


def minus(left, right):
    if right is None:
        return left
    if left is None:
        return -right
    return left - right


def padded_spectrum(blocks):
    m = len(blocks)
    if m == 1:
        return [(blocks[0], None), (blocks[0], None)]
    even = padded_spectrum(blocks[0::2])
    odd = padded_spectrum(blocks[1::2])
    rows = [None] * (m + 1)
    rows[0] = (even[0][0] + odd[0][0], None)
    rows[m] = (even[0][0] - odd[0][0], None)
    for k in range(1, m // 2):
        cos, sin = wave(2 * m, k)
        odd_re, odd_im = odd[k]
        turn_re = odd_re * cos + odd_im * sin
        turn_im = odd_im * cos - odd_re * sin
        rows[k] = (even[k][0] + turn_re, even[k][1] + turn_im)
        rows[m - k] = (even[k][0] - turn_re, turn_im - even[k][1])
    rows[m // 2] = (even[m // 2][0], -odd[m // 2][0])
    return rows


def half_signal(rows):
    m = len(rows) - 1
    if m == 1:
        return [rows[0][0] + rows[1][0]]
    even, odd = [None] * (m // 2 + 1), [None] * (m // 2 + 1)
    even[0] = (rows[0][0] + rows[m][0], None)
    odd[0] = (rows[0][0] - rows[m][0], None)
    for k in range(1, m // 2):
        cos, sin = wave(2 * m, k)
        (low_re, low_im), (top_re, top_im) = rows[k], rows[m - k]
        even[k] = (low_re + top_re, low_im - top_im)
        diff_re, diff_im = low_re - top_re, low_im + top_im
        odd[k] = (diff_re * cos - diff_im * sin, diff_im * cos + diff_re * sin)
    even[m // 2] = (2.0 * rows[m // 2][0], None)
    odd[m // 2] = (-2.0 * rows[m // 2][1], None)
    blocks = [None] * m
    blocks[0::2] = half_signal(even)
    blocks[1::2] = half_signal(odd)
    return blocks


def in_two(table):
    high = table.astype(jnp.bfloat16)
    low = (table - np.asarray(high).astype(np.float64)).astype(jnp.bfloat16)
    return np.stack([np.asarray(high), np.asarray(low)])


def tables(blocks, scale):
    total = 2 * blocks * LANES
    rows = np.arange(blocks + 1)[:, None]
    lanes = np.arange(LANES)[None, :]
    angle = 2.0 * np.pi * (rows * lanes % total) / total
    twist = np.stack([np.cos(angle), -np.sin(angle)]).astype(np.float32)
    untwist = (np.stack([np.cos(angle), np.sin(angle)]) * scale).astype(np.float32)
    turn = 2.0 * np.pi * (lanes.T * lanes % LANES) / LANES
    cos, sin = np.cos(turn), np.sin(turn)
    ahead = in_two(np.block([[cos, -sin], [sin, cos]]))
    back = in_two(np.block([[cos, sin], [-sin, cos]]))
    return twist, untwist, ahead, back


def split_store(high, low, row, part, value):
    top = value.astype(jnp.bfloat16)
    rows = pl.ds(row * CHANS, CHANS)
    cols = pl.ds(part * LANES, LANES)
    high[rows, cols] = top
    low[rows, cols] = (value - top.astype(jnp.float32)).astype(jnp.bfloat16)


def inner(high, low, matrix, out):
    dot = functools.partial(jnp.dot, preferred_element_type=jnp.float32)
    out[...] = (
        dot(high[...], matrix[0]) + dot(low[...], matrix[0]) + dot(high[...], matrix[1])
    )


def cell(spectrum, row):
    rows = pl.ds(row * CHANS, CHANS)
    return spectrum[rows, pl.ds(0, LANES)], spectrum[rows, pl.ds(LANES, LANES)]


def ahead_transform(blocks, twist, matrix, high, low, out):
    for k, (re, im) in enumerate(padded_spectrum(blocks)):
        cos, sin = twist[0, pl.ds(k, 1), :], twist[1, pl.ds(k, 1), :]
        if im is None:
            split_store(high, low, k, 0, re * cos)
            split_store(high, low, k, 1, re * sin)
        else:
            split_store(high, low, k, 0, re * cos - im * sin)
            split_store(high, low, k, 1, re * sin + im * cos)
    inner(high, low, matrix, out)


def back_transform(product, count, untwist, matrix, high, low, out):
    for k in range(count + 1):
        re, im = product(k)
        split_store(high, low, k, 0, re)
        split_store(high, low, k, 1, im)
    inner(high, low, matrix, out)
    rows = []
    for k in range(count + 1):
        cos, sin = untwist[0, pl.ds(k, 1), :], untwist[1, pl.ds(k, 1), :]
        re, im = cell(out, k)
        real = re * cos - im * sin
        rows.append((real, None if k in (0, count) else re * sin + im * cos))
    return half_signal(rows)


def times(left, right):
    return (left[0] * right[0] - left[1] * right[1], left[0] * right[1] + left[1] * right[0])


def times_conj(left, right):
    return (left[0] * right[0] + left[1] * right[1], left[1] * right[0] - left[0] * right[1])


def kernel(
    n_ctx, n_tp, n_dp,
    grad_hbm, gate_hbm, conv_hbm, filt_hbm, weight_hbm,
    twist_hbm, untwist_hbm, ahead_hbm, back_hbm,
    gate_out, conv_grad_out, filt_grad_out,
    ring, gate_buf, conv_buf, filt_buf, weight, twist, untwist, ahead, back,
    unit, gate_send, out_send, grad_send, conv_in, gate_in, out_in, grad_in,
    high, low, spec_filt, spec_conv, spec_gate, spec_tmp, part_send, part_in,
    load_sem, ring_send, ring_recv, swap_send, swap_recv, part_send_sem, part_recv_sem,
):
    ctx, tp, dp = lax.axis_index("ctx"), lax.axis_index("tp"), lax.axis_index("dp")
    right, left = lax.rem(tp + 1, n_tp), lax.rem(tp + n_tp - 1, n_tp)

    barrier = pltpu.get_barrier_semaphore()
    for peer in (right, left):
        pl.semaphore_signal(barrier, inc=1, device_id={"tp": peer}, device_id_type=MESH)

    def greet(i, carry):
        peer = lax.rem(ctx + i, n_ctx)
        pl.semaphore_signal(barrier, inc=1, device_id={"ctx": peer}, device_id_type=MESH)
        return carry

    lax.fori_loop(1, n_ctx, greet, 0)
    for i in range(1, n_dp):
        peer = lax.rem(dp + i, n_dp)
        pl.semaphore_signal(barrier, inc=1, device_id={"dp": peer}, device_id_type=MESH)

    loads = [
        pltpu.make_async_copy(src, dst, load_sem.at[i])
        for i, (src, dst) in enumerate(
            [
                (grad_hbm, ring.at[tp]), (conv_hbm, conv_buf), (filt_hbm, filt_buf),
                (twist_hbm, twist), (ahead_hbm, ahead), (untwist_hbm, untwist),
                (back_hbm, back), (weight_hbm, weight), (gate_hbm, gate_buf),
            ]
        )
    ]
    for load in loads:
        load.start()
    loads[2].wait()
    loads[3].wait()
    loads[4].wait()
    ahead_transform(
        [filt_buf[:, pl.ds(j * LANES, LANES)] for j in range(n_ctx)],
        twist, ahead, high, low, spec_filt,
    )
    loads[0].wait()
    loads[1].wait()
    pl.semaphore_wait(barrier, 2 + n_ctx - 1 + n_dp - 1)

    width = ring.shape[2] // CHUNKS
    last = n_tp // 2 - 1

    def hop(way, step, chunk):
        origin = lax.rem(tp + step, n_tp) if way else lax.rem(tp + n_tp - step, n_tp)
        block = ring.at[origin, :, pl.ds(chunk * width, width)]
        return pltpu.make_async_remote_copy(
            src_ref=block,
            dst_ref=block,
            send_sem=ring_send.at[way, step, chunk],
            recv_sem=ring_recv.at[way, step, chunk],
            device_id={"tp": left if way else right},
            device_id_type=MESH,
        )

    def arrival(way, step, chunk):
        origin = lax.rem(tp + step + 1, n_tp) if way else lax.rem(tp + n_tp - step - 1, n_tp)
        block = ring.at[origin, :, pl.ds(chunk * width, width)]
        return pltpu.make_async_remote_copy(
            src_ref=block,
            dst_ref=block,
            send_sem=ring_send.at[way, step, chunk],
            recv_sem=ring_recv.at[way, step, chunk],
            device_id={"tp": left if way else right},
            device_id_type=MESH,
        )

    def ways(step, chunk):
        if step < last:
            return (0, 1)
        return (0,) if chunk < CHUNKS // 2 else (1,)

    sends = []

    def forward(way, step, chunk):
        copy = hop(way, step, chunk)
        copy.start()
        sends.append(copy)

    for chunk in range(CHUNKS):
        for way in ways(0, chunk):
            forward(way, 0, chunk)

    mine = pl.ds(pl.multiple_of(ctx * CHANS, CHANS), CHANS)

    def exchange(which, source, target):
        def send(i, carry):
            peer = lax.rem(ctx + i, n_ctx)
            theirs = pl.ds(pl.multiple_of(peer * CHANS, CHANS), CHANS)
            pltpu.make_async_remote_copy(
                src_ref=source.at[theirs, :],
                dst_ref=target.at[mine, :],
                send_sem=swap_send.at[which],
                recv_sem=swap_recv.at[which],
                device_id={"ctx": peer},
                device_id_type=MESH,
            ).start()
            return carry

        lax.fori_loop(1, n_ctx, send, 0)
        target[mine, :] = source[mine, :]

    def exchanged(which, source, target):
        rows = pl.ds(0, (n_ctx - 1) * CHANS)
        return pltpu.make_async_remote_copy(
            src_ref=source.at[rows, :],
            dst_ref=target.at[rows, :],
            send_sem=swap_send.at[which],
            recv_sem=swap_recv.at[which],
            device_id={"ctx": lax.rem(ctx + 1, n_ctx)},
            device_id_type=MESH,
        )

    def token_blocks(buf):
        return [
            buf[pl.ds(j * CHANS, CHANS), :].astype(jnp.float32) for j in range(n_ctx)
        ]

    def put_blocks(buf, blocks):
        for j, block in enumerate(blocks):
            buf[pl.ds(j * CHANS, CHANS), :] = block.astype(jnp.bfloat16)

    exchange(0, conv_buf, conv_in)

    for step in range(last):
        for chunk in range(CHUNKS):
            for way in (0, 1):
                arrival(way, step, chunk).wait_recv()
                if way in ways(step + 1, chunk):
                    forward(way, step + 1, chunk)
    for chunk in range(CHUNKS):
        for way in ways(last, chunk):
            arrival(way, last, chunk).wait_recv()

    loads[7].wait()
    loads[8].wait()
    tokens = ring[...].reshape(LANES, ring.shape[2])
    tile = min(128, unit.shape[0])

    def project(i, carry):
        rows = pl.ds(pl.multiple_of(i * tile, tile), tile)
        grad = lax.dot_general(
            weight[rows, :], tokens, (((1,), (1,)), ((), ())),
            preferred_element_type=jnp.float32,
        )
        unit[rows, :] = grad
        gate_send[rows, :] = (grad * gate_buf[rows, :].astype(jnp.float32)).astype(jnp.bfloat16)
        return carry

    lax.fori_loop(0, unit.shape[0] // tile, project, 0)
    exchange(1, gate_send, gate_in)

    exchanged(0, conv_buf, conv_in).wait_recv()
    ahead_transform(token_blocks(conv_in), twist, ahead, high, low, spec_conv)
    loads[5].wait()
    loads[6].wait()
    put_blocks(out_send, back_transform(
        lambda k: times(cell(spec_filt, k), cell(spec_conv, k)),
        n_ctx, untwist, back, high, low, spec_tmp,
    ))
    exchange(2, out_send, out_in)

    exchanged(1, gate_send, gate_in).wait_recv()
    ahead_transform(token_blocks(gate_in), twist, ahead, high, low, spec_gate)
    put_blocks(grad_send, back_transform(
        lambda k: times_conj(cell(spec_gate, k), cell(spec_filt, k)),
        n_ctx, untwist, back, high, low, spec_tmp,
    ))
    exchange(3, grad_send, grad_in)

    per = CHANS // n_dp
    group = 8 // per
    filt_grads = back_transform(
        lambda k: times_conj(cell(spec_gate, k), cell(spec_conv, k)),
        n_ctx, untwist, back, high, low, spec_tmp,
    )
    for piece in range(n_dp):
        for j, block in enumerate(filt_grads):
            part_send[piece, j // group, pl.ds(j % group * per, per), :] = block[
                piece * per : (piece + 1) * per, :
            ]

    def part(i):
        peer = lax.rem(dp + i, n_dp)
        return pltpu.make_async_remote_copy(
            src_ref=part_send.at[peer],
            dst_ref=part_in.at[i - 1],
            send_sem=part_send_sem.at[i - 1],
            recv_sem=part_recv_sem.at[i - 1],
            device_id={"dp": peer},
            device_id_type=MESH,
        )

    parts = [part(i) for i in range(1, n_dp)]
    for copy in parts:
        copy.start()

    exchanged(2, out_send, out_in).wait_recv()
    gate_out[...] = (unit[...] * out_in[...].astype(jnp.float32)).astype(jnp.bfloat16)

    for copy in parts:
        copy.wait_recv()
    total = part_send[dp]
    for i in range(n_dp - 1):
        total = total + part_in[i]
    for j in range(n_ctx):
        filt_grad_out[:, pl.ds(j * LANES, LANES)] = total[
            j // group, j % group * per : (j % group + 1) * per, :
        ]

    exchanged(3, grad_send, grad_in).wait_recv()
    conv_grad_out[...] = grad_in[...]

    for copy in sends:
        copy.wait_send()
    for which, source, target in (
        (0, conv_buf, conv_in), (1, gate_send, gate_in),
        (2, out_send, out_in), (3, grad_send, grad_in),
    ):
        exchanged(which, source, target).wait_send()
    for copy in parts:
        copy.wait_send()


def on_device(sizes, out_grad, gate_in, conv_in, filter_raw, out_weight):
    n_ctx, n_tp, n_dp = sizes
    bf16, f32 = jnp.bfloat16, jnp.float32
    length = filter_raw.shape[1]
    depth = out_weight.shape[1]
    local = gate_in.shape[1]
    scale = 1.0 / math.sqrt(length) / (2 * length)
    twist, untwist, ahead, back = tables(n_ctx, scale)
    rows = (n_ctx + 1) * CHANS
    per = CHANS // n_dp
    group = 8 // per
    vmem = pltpu.VMEM
    dma = pltpu.SemaphoreType.DMA
    whole = pl.BlockSpec(memory_space=pltpu.VMEM)
    grad, gate, filt = pl.pallas_call(
        functools.partial(kernel, n_ctx, n_tp, n_dp),
        out_shape=(
            jax.ShapeDtypeStruct((local, LANES), bf16),
            jax.ShapeDtypeStruct((local, LANES), bf16),
            jax.ShapeDtypeStruct((per, length), f32),
        ),
        in_specs=[pl.BlockSpec(memory_space=pl.ANY)] * 9,
        out_specs=(whole, whole, whole),
        scratch_shapes=[
            vmem((n_tp, 16, depth), bf16),
            vmem((local, LANES), bf16),
            vmem((local, LANES), bf16),
            vmem((CHANS, length), f32),
            vmem((local, depth), bf16),
            vmem(twist.shape, f32),
            vmem(untwist.shape, f32),
            vmem(ahead.shape, bf16),
            vmem(back.shape, bf16),
            vmem((local, LANES), f32),
            *[vmem((local, LANES), bf16)] * 7,
            vmem((rows, 2 * LANES), bf16),
            vmem((rows, 2 * LANES), bf16),
            *[vmem((rows, 2 * LANES), f32)] * 4,
            vmem((n_dp, n_ctx // group, 8, LANES), f32),
            vmem((n_dp - 1, n_ctx // group, 8, LANES), f32),
            dma((9,)),
            dma((2, n_tp // 2, CHUNKS)),
            dma((2, n_tp // 2, CHUNKS)),
            dma((4,)),
            dma((4,)),
            dma((n_dp - 1,)),
            dma((n_dp - 1,)),
        ],
        compiler_params=pltpu.CompilerParams(collective_id=0, has_side_effects=True),
    )(
        out_grad[0], gate_in[0], conv_in[0], filter_raw, out_weight,
        jnp.asarray(twist), jnp.asarray(untwist), jnp.asarray(ahead), jnp.asarray(back),
    )
    return grad[None], gate[None], filt


def solution(mesh):
    sizes = (mesh.shape["ctx"], mesh.shape["tp"], mesh.shape["dp"])
    placed = (
        P("dp", ("ctx", "tp"), None),
        P("dp", "tp", "ctx"),
        P("dp", "tp", "ctx"),
        P(("tp", "ctx"), None),
        P("tp", None),
    )
    return jax.shard_map(
        functools.partial(on_device, sizes),
        mesh=mesh,
        in_specs=placed,
        out_specs=(P("dp", "tp", "ctx"), P("dp", "tp", "ctx"), P(("tp", "ctx", "dp"), None)),
        check_vma=False,
    )
```

```python
import functools
import math

import jax
import jax.numpy as jnp
import numpy as np
from jax import lax
from jax.experimental import pallas as pl
from jax.experimental.pallas import tpu as pltpu
from jax.sharding import PartitionSpec as P

MESH = pl.DeviceIdType.MESH
LANES = 128
CHANS = 16
CHUNKS = 4
FINISH_VMEM = 1024 * 1024
MAIN_VMEM = 65536000


def wave(order, index):
    angle = 2.0 * math.pi * (index % order) / order
    return (math.cos(angle), math.sin(angle))


def plus(left, right):
    if left is None:
        return right
    if right is None:
        return left
    return left + right


def minus(left, right):
    if right is None:
        return left
    if left is None:
        return -right
    return left - right


def padded_spectrum(blocks):
    m = len(blocks)
    if m == 1:
        return [(blocks[0], None), (blocks[0], None)]
    even = padded_spectrum(blocks[0::2])
    odd = padded_spectrum(blocks[1::2])
    rows = [None] * (m + 1)
    rows[0] = (even[0][0] + odd[0][0], None)
    rows[m] = (even[0][0] - odd[0][0], None)
    for k in range(1, m // 2):
        cos, sin = wave(2 * m, k)
        odd_re, odd_im = odd[k]
        turn_re = odd_re * cos + odd_im * sin
        turn_im = odd_im * cos - odd_re * sin
        rows[k] = (even[k][0] + turn_re, even[k][1] + turn_im)
        rows[m - k] = (even[k][0] - turn_re, turn_im - even[k][1])
    rows[m // 2] = (even[m // 2][0], -odd[m // 2][0])
    return rows


def half_signal(rows):
    m = len(rows) - 1
    if m == 1:
        return [rows[0][0] + rows[1][0]]
    even, odd = [None] * (m // 2 + 1), [None] * (m // 2 + 1)
    even[0] = (rows[0][0] + rows[m][0], None)
    odd[0] = (rows[0][0] - rows[m][0], None)
    for k in range(1, m // 2):
        cos, sin = wave(2 * m, k)
        (low_re, low_im), (top_re, top_im) = rows[k], rows[m - k]
        even[k] = (low_re + top_re, low_im - top_im)
        diff_re, diff_im = low_re - top_re, low_im + top_im
        odd[k] = (diff_re * cos - diff_im * sin, diff_im * cos + diff_re * sin)
    even[m // 2] = (2.0 * rows[m // 2][0], None)
    odd[m // 2] = (-2.0 * rows[m // 2][1], None)
    blocks = [None] * m
    blocks[0::2] = half_signal(even)
    blocks[1::2] = half_signal(odd)
    return blocks


def in_two(table):
    high = table.astype(jnp.bfloat16)
    low = (table - np.asarray(high).astype(np.float64)).astype(jnp.bfloat16)
    return np.stack([np.asarray(high), np.asarray(low)])


def tables(blocks, scale):
    total = 2 * blocks * LANES
    rows = np.arange(blocks + 1)[:, None]
    lanes = np.arange(LANES)[None, :]
    angle = 2.0 * np.pi * (rows * lanes % total) / total
    twist = np.stack([np.cos(angle), -np.sin(angle)]).astype(np.float32)
    untwist = (np.stack([np.cos(angle), np.sin(angle)]) * scale).astype(np.float32)
    turn = 2.0 * np.pi * (lanes.T * lanes % LANES) / LANES
    cos, sin = np.cos(turn), np.sin(turn)
    ahead = in_two(np.block([[cos, -sin], [sin, cos]]))
    back = in_two(np.block([[cos, sin], [-sin, cos]]))
    return twist, untwist, ahead, back


def split_store(high, low, row, part, value):
    top = value.astype(jnp.bfloat16)
    rows = pl.ds(row * CHANS, CHANS)
    cols = pl.ds(part * LANES, LANES)
    high[rows, cols] = top
    low[rows, cols] = (value - top.astype(jnp.float32)).astype(jnp.bfloat16)


def inner(high, low, matrix, out):
    dot = functools.partial(jnp.dot, preferred_element_type=jnp.float32)
    out[...] = (
        dot(high[...], matrix[0]) + dot(low[...], matrix[0]) + dot(high[...], matrix[1])
    )


def cell(spectrum, row):
    rows = pl.ds(row * CHANS, CHANS)
    return spectrum[rows, pl.ds(0, LANES)], spectrum[rows, pl.ds(LANES, LANES)]


def ahead_transform(blocks, twist, matrix, high, low, out):
    for k, (re, im) in enumerate(padded_spectrum(blocks)):
        cos, sin = twist[0, pl.ds(k, 1), :], twist[1, pl.ds(k, 1), :]
        if im is None:
            split_store(high, low, k, 0, re * cos)
            split_store(high, low, k, 1, re * sin)
        else:
            split_store(high, low, k, 0, re * cos - im * sin)
            split_store(high, low, k, 1, re * sin + im * cos)
    inner(high, low, matrix, out)


def back_transform(product, count, untwist, matrix, high, low, out):
    for k in range(count + 1):
        re, im = product(k)
        split_store(high, low, k, 0, re)
        split_store(high, low, k, 1, im)
    inner(high, low, matrix, out)
    rows = []
    for k in range(count + 1):
        cos, sin = untwist[0, pl.ds(k, 1), :], untwist[1, pl.ds(k, 1), :]
        re, im = cell(out, k)
        real = re * cos - im * sin
        rows.append((real, None if k in (0, count) else re * sin + im * cos))
    return half_signal(rows)


def times(left, right):
    return (left[0] * right[0] - left[1] * right[1], left[0] * right[1] + left[1] * right[0])


def times_conj(left, right):
    return (left[0] * right[0] + left[1] * right[1], left[1] * right[0] - left[0] * right[1])


def kernel(
    n_ctx, n_tp, n_dp,
    grad_hbm, gate_hbm, conv_hbm, filt_hbm, weight_hbm,
    twist_hbm, untwist_hbm, ahead_hbm, back_hbm,
    gate_out, conv_grad_out, filt_grad_out,
    ring, gate_buf, conv_buf, filt_buf, weight, twist, untwist, ahead, back,
    unit, gate_send, out_send, grad_send, conv_in, gate_in, out_in, grad_in,
    high, low, spec_filt, spec_conv, spec_gate, spec_tmp, part_send, part_in,
    load_sem, ring_send, ring_recv, swap_send, swap_recv, part_send_sem, part_recv_sem,
    news,
):
    ctx, tp, dp = lax.axis_index("ctx"), lax.axis_index("tp"), lax.axis_index("dp")
    right, left = lax.rem(tp + 1, n_tp), lax.rem(tp + n_tp - 1, n_tp)

    n_y, n_z = n_ctx // 4, 2 * n_dp
    y, z, core = ctx // 4, lax.rem(ctx // 2, 2) * n_dp + dp, lax.rem(ctx, 2)

    def place(y_at, z_at, core_at):
        return {"ctx": y_at * 4 + z_at // n_dp * 2 + core_at, "dp": lax.rem(z_at, n_dp)}

    y_sides = [place(lax.rem(y + d, n_y), z, core) for d in (1, n_y - 1)]
    z_sides = [place(y, lax.rem(z + d, n_z), core) for d in (1, n_z - 1)]
    other_core = [place(y, z, 1 - core)]
    tp_sides = [{"tp": right}, {"tp": left}]

    barrier = pltpu.get_barrier_semaphore()
    close_by = tp_sides + y_sides + z_sides + other_core
    for peer in close_by:
        pl.semaphore_signal(barrier, inc=1, device_id=peer, device_id_type=MESH)
    rounds = [y_sides] * (n_y // 2 - 1) + [z_sides] * (n_z // 2) + [other_core]

    def tell(at):
        for peer in rounds[at]:
            pl.semaphore_signal(news.at[at], inc=1, device_id=peer, device_id_type=MESH)

    def hear(at):
        pl.semaphore_wait(news.at[at], len(rounds[at]))
        if at + 1 < len(rounds):
            tell(at + 1)

    loads = [
        pltpu.make_async_copy(src, dst, load_sem.at[i])
        for i, (src, dst) in enumerate(
            [
                (grad_hbm, ring.at[tp]), (conv_hbm, conv_buf), (filt_hbm, filt_buf),
                (twist_hbm, twist), (ahead_hbm, ahead), (untwist_hbm, untwist),
                (back_hbm, back), (weight_hbm, weight), (gate_hbm, gate_buf),
            ]
        )
    ]
    for load in loads:
        load.start()
    pl.semaphore_wait(barrier, len(close_by))

    width = ring.shape[2] // CHUNKS
    last = n_tp // 2 - 1

    def hop(way, step, chunk):
        origin = lax.rem(tp + step, n_tp) if way else lax.rem(tp + n_tp - step, n_tp)
        cols = pl.ds(chunk * width, width)
        block = ring.at[origin, :, cols]
        return pltpu.make_async_remote_copy(
            src_ref=block if step else grad_hbm.at[:, cols],
            dst_ref=block,
            send_sem=ring_send.at[way, step, chunk],
            recv_sem=ring_recv.at[way, step, chunk],
            device_id={"tp": left if way else right},
            device_id_type=MESH,
        )

    def arrival(way, step, chunk):
        origin = lax.rem(tp + step + 1, n_tp) if way else lax.rem(tp + n_tp - step - 1, n_tp)
        block = ring.at[origin, :, pl.ds(chunk * width, width)]
        return pltpu.make_async_remote_copy(
            src_ref=block,
            dst_ref=block,
            send_sem=ring_send.at[way, step, chunk],
            recv_sem=ring_recv.at[way, step, chunk],
            device_id={"tp": left if way else right},
            device_id_type=MESH,
        )

    def ways(step, chunk):
        if step < last:
            return (0, 1)
        return (0,) if chunk < CHUNKS // 2 else (1,)

    sends = []

    def forward(way, step, chunk):
        copy = hop(way, step, chunk)
        copy.start()
        sends.append(copy)

    for chunk in range(CHUNKS):
        for way in ways(0, chunk):
            forward(way, 0, chunk)
    tell(0)

    loads[2].wait()
    loads[3].wait()
    loads[4].wait()
    ahead_transform(
        [filt_buf[:, pl.ds(j * LANES, LANES)] for j in range(n_ctx)],
        twist, ahead, high, low, spec_filt,
    )
    loads[0].wait()
    loads[1].wait()

    mine = pl.ds(pl.multiple_of(ctx * CHANS, CHANS), CHANS)

    def exchange(which, source, target):
        def send(i, carry):
            peer = lax.rem(ctx + i, n_ctx)
            theirs = pl.ds(pl.multiple_of(peer * CHANS, CHANS), CHANS)
            pltpu.make_async_remote_copy(
                src_ref=source.at[theirs, :],
                dst_ref=target.at[mine, :],
                send_sem=swap_send.at[which],
                recv_sem=swap_recv.at[which],
                device_id={"ctx": peer},
                device_id_type=MESH,
            ).start()
            return carry

        lax.fori_loop(1, n_ctx, send, 0)
        target[mine, :] = source[mine, :]

    def exchanged(which, source, target):
        rows = pl.ds(0, (n_ctx - 1) * CHANS)
        return pltpu.make_async_remote_copy(
            src_ref=source.at[rows, :],
            dst_ref=target.at[rows, :],
            send_sem=swap_send.at[which],
            recv_sem=swap_recv.at[which],
            device_id={"ctx": lax.rem(ctx + 1, n_ctx)},
            device_id_type=MESH,
        )

    def token_blocks(buf):
        return [
            buf[pl.ds(j * CHANS, CHANS), :].astype(jnp.float32) for j in range(n_ctx)
        ]

    def put_blocks(buf, blocks):
        for j, block in enumerate(blocks):
            buf[pl.ds(j * CHANS, CHANS), :] = block.astype(jnp.bfloat16)

    heard = 0
    for step in range(last):
        for chunk in range(CHUNKS):
            for way in (0, 1):
                arrival(way, step, chunk).wait_recv()
                if way in ways(step + 1, chunk):
                    forward(way, step + 1, chunk)
            if heard < len(rounds):
                hear(heard)
                heard += 1
                if heard == len(rounds):
                    exchange(0, conv_buf, conv_in)
    for chunk in range(CHUNKS):
        for way in ways(last, chunk):
            arrival(way, last, chunk).wait_recv()

    loads[7].wait()
    loads[8].wait()
    tokens = ring[...].reshape(LANES, ring.shape[2])
    tile = min(128, unit.shape[0])

    def project(i, carry):
        rows = pl.ds(pl.multiple_of(i * tile, tile), tile)
        grad = lax.dot_general(
            weight[rows, :], tokens, (((1,), (1,)), ((), ())),
            preferred_element_type=jnp.float32,
        )
        unit[rows, :] = grad
        gate_send[rows, :] = (grad * gate_buf[rows, :].astype(jnp.float32)).astype(jnp.bfloat16)
        return carry

    lax.fori_loop(0, unit.shape[0] // tile, project, 0)
    exchange(1, gate_send, gate_in)

    exchanged(0, conv_buf, conv_in).wait_recv()
    ahead_transform(token_blocks(conv_in), twist, ahead, high, low, spec_conv)
    loads[5].wait()
    loads[6].wait()
    put_blocks(out_send, back_transform(
        lambda k: times(cell(spec_filt, k), cell(spec_conv, k)),
        n_ctx, untwist, back, high, low, spec_tmp,
    ))
    exchange(2, out_send, out_in)

    exchanged(1, gate_send, gate_in).wait_recv()
    ahead_transform(token_blocks(gate_in), twist, ahead, high, low, spec_gate)
    put_blocks(grad_send, back_transform(
        lambda k: times_conj(cell(spec_gate, k), cell(spec_filt, k)),
        n_ctx, untwist, back, high, low, spec_tmp,
    ))
    exchange(3, grad_send, grad_in)

    per = CHANS // n_dp
    group = max(8 // per, 1)
    filt_grads = back_transform(
        lambda k: times_conj(cell(spec_gate, k), cell(spec_conv, k)),
        n_ctx, untwist, back, high, low, spec_tmp,
    )
    for piece in range(n_dp):
        for j, block in enumerate(filt_grads):
            part_send[piece, j // group, pl.ds(j % group * per, per), :] = block[
                piece * per : (piece + 1) * per, :
            ]

    def part(i):
        peer = lax.rem(dp + i, n_dp)
        return pltpu.make_async_remote_copy(
            src_ref=part_send.at[peer],
            dst_ref=part_in.at[i - 1],
            send_sem=part_send_sem.at[i - 1],
            recv_sem=part_recv_sem.at[i - 1],
            device_id={"dp": peer},
            device_id_type=MESH,
        )

    parts = [part(i) for i in range(1, n_dp)]
    for copy in parts:
        copy.start()

    exchanged(2, out_send, out_in).wait_recv()
    gate_out[...] = (unit[...] * out_in[...].astype(jnp.float32)).astype(jnp.bfloat16)

    for copy in parts:
        copy.wait_recv()
    total = part_send[dp]
    for i in range(n_dp - 1):
        total = total + part_in[i]
    for j in range(n_ctx):
        filt_grad_out[:, pl.ds(j * LANES, LANES)] = total[
            j // group, j % group * per : (j % group + 1) * per, :
        ]

    exchanged(3, grad_send, grad_in).wait_recv()
    conv_grad_out[...] = grad_in[...]

    for copy in sends:
        copy.wait_send()
    for which, source, target in (
        (0, conv_buf, conv_in), (1, gate_send, gate_in),
        (2, out_send, out_in), (3, grad_send, grad_in),
    ):
        exchanged(which, source, target).wait_send()
    for copy in parts:
        copy.wait_send()


def hand_over(*refs):
    half = len(refs) // 2
    copies = [
        pltpu.make_async_copy(refs[i], refs[half + i], refs[-1].at[i]) for i in range(half)
    ]
    for copy in copies:
        copy.start()
    for copy in copies:
        copy.wait()


def on_device(sizes, out_grad, gate_in, conv_in, filter_raw, out_weight):
    n_ctx, n_tp, n_dp = sizes
    bf16, f32 = jnp.bfloat16, jnp.float32
    length = filter_raw.shape[1]
    depth = out_weight.shape[1]
    local = gate_in.shape[1]
    scale = 1.0 / math.sqrt(length) / (2 * length)
    twist, untwist, ahead, back = tables(n_ctx, scale)
    rows = (n_ctx + 1) * CHANS
    per = CHANS // n_dp
    group = max(8 // per, 1)
    vmem = pltpu.VMEM
    dma = pltpu.SemaphoreType.DMA
    whole = pl.BlockSpec(memory_space=pltpu.VMEM)
    grad, gate, filt = pl.pallas_call(
        functools.partial(kernel, n_ctx, n_tp, n_dp),
        out_shape=(
            jax.ShapeDtypeStruct((local, LANES), bf16),
            jax.ShapeDtypeStruct((local, LANES), bf16),
            jax.ShapeDtypeStruct((per, length), f32),
        ),
        in_specs=[pl.BlockSpec(memory_space=pltpu.HBM)] * 9,
        out_specs=(whole, whole, whole),
        scratch_shapes=[
            vmem((n_tp, 16, depth), bf16),
            vmem((local, LANES), bf16),
            vmem((local, LANES), bf16),
            vmem((CHANS, length), f32),
            vmem((local, depth), bf16),
            vmem(twist.shape, f32),
            vmem(untwist.shape, f32),
            vmem(ahead.shape, bf16),
            vmem(back.shape, bf16),
            vmem((local, LANES), f32),
            *[vmem((local, LANES), bf16)] * 7,
            vmem((rows, 2 * LANES), bf16),
            vmem((rows, 2 * LANES), bf16),
            *[vmem((rows, 2 * LANES), f32)] * 4,
            vmem((n_dp, n_ctx // group, 8, LANES), f32),
            vmem((n_dp - 1, n_ctx // group, 8, LANES), f32),
            dma((9,)),
            dma((2, n_tp // 2, CHUNKS)),
            dma((2, n_tp // 2, CHUNKS)),
            dma((4,)),
            dma((4,)),
            dma((n_dp - 1,)),
            dma((n_dp - 1,)),
            pltpu.SemaphoreType.REGULAR((n_ctx // 8 - 1 + n_dp + 1,)),
        ],
        compiler_params=pltpu.CompilerParams(
            collective_id=0, has_side_effects=True, vmem_limit_bytes=MAIN_VMEM
        ),
    )(
        out_grad[0], gate_in[0], conv_in[0], filter_raw, out_weight,
        jnp.asarray(twist), jnp.asarray(untwist), jnp.asarray(ahead), jnp.asarray(back),
    )
    grad, gate, filt = pl.pallas_call(
        hand_over,
        out_shape=tuple(jax.ShapeDtypeStruct(a.shape, a.dtype) for a in (grad, gate, filt)),
        in_specs=[pl.BlockSpec(memory_space=pl.ANY)] * 3,
        out_specs=(pl.BlockSpec(memory_space=pltpu.HBM),) * 3,
        scratch_shapes=[dma((3,))],
        compiler_params=pltpu.CompilerParams(vmem_limit_bytes=FINISH_VMEM),
    )(grad, gate, filt)
    return grad[None], gate[None], filt


def solution(mesh):
    sizes = (mesh.shape["ctx"], mesh.shape["tp"], mesh.shape["dp"])
    placed = (
        P("dp", ("ctx", "tp"), None),
        P("dp", "tp", "ctx"),
        P("dp", "tp", "ctx"),
        P(("tp", "ctx"), None),
        P("tp", None),
    )
    return jax.shard_map(
        functools.partial(on_device, sizes),
        mesh=mesh,
        in_specs=placed,
        out_specs=(P("dp", "tp", "ctx"), P("dp", "tp", "ctx"), P(("tp", "ctx", "dp"), None)),
        check_vma=False,
    )
```

```python
import functools
import math

import jax
import jax.numpy as jnp
import numpy as np
from jax import lax
from jax.experimental import pallas as pl
from jax.experimental.pallas import tpu as pltpu
from jax.sharding import PartitionSpec as P

MESH = pl.DeviceIdType.MESH
LANES = 128
CHANS = 16
CHUNKS = 4
FINISH_VMEM = 1024 * 1024
MAIN_VMEM = 64000 * 1024


def wave(order, index):
    angle = 2.0 * math.pi * (index % order) / order
    return (math.cos(angle), math.sin(angle))


def plus(left, right):
    if left is None:
        return right
    if right is None:
        return left
    return left + right


def minus(left, right):
    if right is None:
        return left
    if left is None:
        return -right
    return left - right


def padded_spectrum(blocks):
    m = len(blocks)
    if m == 1:
        return [(blocks[0], None), (blocks[0], None)]
    even = padded_spectrum(blocks[0::2])
    odd = padded_spectrum(blocks[1::2])
    rows = [None] * (m + 1)
    rows[0] = (even[0][0] + odd[0][0], None)
    rows[m] = (even[0][0] - odd[0][0], None)
    for k in range(1, m // 2):
        cos, sin = wave(2 * m, k)
        odd_re, odd_im = odd[k]
        turn_re = odd_re * cos + odd_im * sin
        turn_im = odd_im * cos - odd_re * sin
        rows[k] = (even[k][0] + turn_re, even[k][1] + turn_im)
        rows[m - k] = (even[k][0] - turn_re, turn_im - even[k][1])
    rows[m // 2] = (even[m // 2][0], -odd[m // 2][0])
    return rows


def half_signal(rows):
    m = len(rows) - 1
    if m == 1:
        return [rows[0][0] + rows[1][0]]
    even, odd = [None] * (m // 2 + 1), [None] * (m // 2 + 1)
    even[0] = (rows[0][0] + rows[m][0], None)
    odd[0] = (rows[0][0] - rows[m][0], None)
    for k in range(1, m // 2):
        cos, sin = wave(2 * m, k)
        (low_re, low_im), (top_re, top_im) = rows[k], rows[m - k]
        even[k] = (low_re + top_re, low_im - top_im)
        diff_re, diff_im = low_re - top_re, low_im + top_im
        odd[k] = (diff_re * cos - diff_im * sin, diff_im * cos + diff_re * sin)
    even[m // 2] = (2.0 * rows[m // 2][0], None)
    odd[m // 2] = (-2.0 * rows[m // 2][1], None)
    blocks = [None] * m
    blocks[0::2] = half_signal(even)
    blocks[1::2] = half_signal(odd)
    return blocks


def in_two(table):
    high = table.astype(jnp.bfloat16)
    low = (table - np.asarray(high).astype(np.float64)).astype(jnp.bfloat16)
    return np.stack([np.asarray(high), np.asarray(low)])


def tables(blocks, scale):
    total = 2 * blocks * LANES
    rows = np.arange(blocks + 1)[:, None]
    lanes = np.arange(LANES)[None, :]
    angle = 2.0 * np.pi * (rows * lanes % total) / total
    twist = np.stack([np.cos(angle), -np.sin(angle)]).astype(np.float32)
    untwist = (np.stack([np.cos(angle), np.sin(angle)]) * scale).astype(np.float32)
    turn = 2.0 * np.pi * (lanes.T * lanes % LANES) / LANES
    cos, sin = np.cos(turn), np.sin(turn)
    ahead = in_two(np.block([[cos, -sin], [sin, cos]]))
    back = in_two(np.block([[cos, sin], [-sin, cos]]))
    return twist, untwist, ahead, back


def split_store(high, low, row, part, value):
    top = value.astype(jnp.bfloat16)
    rows = pl.ds(row * CHANS, CHANS)
    cols = pl.ds(part * LANES, LANES)
    high[rows, cols] = top
    low[rows, cols] = (value - top.astype(jnp.float32)).astype(jnp.bfloat16)


def inner(high, low, matrix, out):
    dot = functools.partial(jnp.dot, preferred_element_type=jnp.float32)
    out[...] = (
        dot(high[...], matrix[0]) + dot(low[...], matrix[0]) + dot(high[...], matrix[1])
    )


def cell(spectrum, row):
    rows = pl.ds(row * CHANS, CHANS)
    return spectrum[rows, pl.ds(0, LANES)], spectrum[rows, pl.ds(LANES, LANES)]


def ahead_transform(blocks, twist, matrix, high, low, out):
    for k, (re, im) in enumerate(padded_spectrum(blocks)):
        cos, sin = twist[0, pl.ds(k, 1), :], twist[1, pl.ds(k, 1), :]
        if im is None:
            split_store(high, low, k, 0, re * cos)
            split_store(high, low, k, 1, re * sin)
        else:
            split_store(high, low, k, 0, re * cos - im * sin)
            split_store(high, low, k, 1, re * sin + im * cos)
    inner(high, low, matrix, out)


def back_transform(product, count, untwist, matrix, high, low, out):
    for k in range(count + 1):
        re, im = product(k)
        split_store(high, low, k, 0, re)
        split_store(high, low, k, 1, im)
    inner(high, low, matrix, out)
    rows = []
    for k in range(count + 1):
        cos, sin = untwist[0, pl.ds(k, 1), :], untwist[1, pl.ds(k, 1), :]
        re, im = cell(out, k)
        real = re * cos - im * sin
        rows.append((real, None if k in (0, count) else re * sin + im * cos))
    return half_signal(rows)


def times(left, right):
    return (left[0] * right[0] - left[1] * right[1], left[0] * right[1] + left[1] * right[0])


def times_conj(left, right):
    return (left[0] * right[0] + left[1] * right[1], left[1] * right[0] - left[0] * right[1])


def kernel(
    n_ctx, n_tp, n_dp,
    grad_hbm, gate_hbm, conv_hbm, filt_hbm, weight_hbm,
    twist_hbm, untwist_hbm, ahead_hbm, back_hbm,
    gate_out, conv_grad_out, filt_grad_out,
    ring, gate_buf, conv_buf, filt_buf, weight, twist, untwist, ahead, back,
    unit, gate_send, out_send, grad_send, conv_in, gate_in, out_in, grad_in,
    high, low, spec_filt, spec_conv, spec_gate, spec_tmp, part_own, part_send, part_in,
    load_sem, ring_send, ring_recv, swap_send, swap_recv, part_send_sem, part_recv_sem,
    news,
):
    ctx, tp, dp = lax.axis_index("ctx"), lax.axis_index("tp"), lax.axis_index("dp")
    right, left = lax.rem(tp + 1, n_tp), lax.rem(tp + n_tp - 1, n_tp)

    n_y, n_z = n_ctx // 4, 2 * n_dp
    y, z, core = ctx // 4, lax.rem(ctx // 2, 2) * n_dp + dp, lax.rem(ctx, 2)

    def place(y_at, z_at, core_at):
        return {"ctx": y_at * 4 + z_at // n_dp * 2 + core_at, "dp": lax.rem(z_at, n_dp)}

    z_line = [place(y, lax.rem(z + d, n_z), core) for d in range(1, n_z)]
    y_lines = [
        place(lax.rem(y + d, n_y), z, lax.rem(core + c, 2))
        for d in range(n_y) for c in (0, 1) if d or c
    ]

    barrier = pltpu.get_barrier_semaphore()
    first = [{"tp": right}, {"tp": left}] + y_lines + z_line
    for peer in first:
        pl.semaphore_signal(barrier, inc=1, device_id=peer, device_id_type=MESH)

    loads = [
        pltpu.make_async_copy(src, dst, load_sem.at[i])
        for i, (src, dst) in enumerate(
            [
                (grad_hbm, ring.at[tp]), (conv_hbm, conv_buf), (filt_hbm, filt_buf),
                (twist_hbm, twist), (ahead_hbm, ahead), (untwist_hbm, untwist),
                (back_hbm, back), (weight_hbm, weight), (gate_hbm, gate_buf),
            ]
        )
    ]
    for load in loads:
        load.start()
    pl.semaphore_wait(barrier, len(first))

    width = ring.shape[2] // CHUNKS
    last = n_tp // 2 - 1

    def hop(way, step, chunk):
        origin = lax.rem(tp + step, n_tp) if way else lax.rem(tp + n_tp - step, n_tp)
        cols = pl.ds(chunk * width, width)
        block = ring.at[origin, :, cols]
        return pltpu.make_async_remote_copy(
            src_ref=block if step else grad_hbm.at[:, cols],
            dst_ref=block,
            send_sem=ring_send.at[way, step, chunk],
            recv_sem=ring_recv.at[way, step, chunk],
            device_id={"tp": left if way else right},
            device_id_type=MESH,
        )

    def arrival(way, step, chunk):
        origin = lax.rem(tp + step + 1, n_tp) if way else lax.rem(tp + n_tp - step - 1, n_tp)
        block = ring.at[origin, :, pl.ds(chunk * width, width)]
        return pltpu.make_async_remote_copy(
            src_ref=block,
            dst_ref=block,
            send_sem=ring_send.at[way, step, chunk],
            recv_sem=ring_recv.at[way, step, chunk],
            device_id={"tp": left if way else right},
            device_id_type=MESH,
        )

    def ways(step, chunk):
        if step < last:
            return (0, 1)
        return (0,) if chunk < CHUNKS // 2 else (1,)

    orders = (range(CHUNKS), [(c + CHUNKS // 2) % CHUNKS for c in range(CHUNKS)])
    sends = []

    def forward(way, step, chunk):
        copy = hop(way, step, chunk)
        copy.start()
        sends.append(copy)

    for turn in range(CHUNKS):
        for way in (0, 1):
            forward(way, 0, orders[way][turn])
    for peer in z_line:
        pl.semaphore_signal(news, inc=1, device_id=peer, device_id_type=MESH)

    loads[2].wait()
    loads[3].wait()
    loads[4].wait()
    ahead_transform(
        [filt_buf[:, pl.ds(j * LANES, LANES)] for j in range(n_ctx)],
        twist, ahead, high, low, spec_filt,
    )
    loads[0].wait()
    loads[1].wait()

    mine = pl.ds(pl.multiple_of(ctx * CHANS, CHANS), CHANS)

    def exchange(which, source, target):
        def send(i, carry):
            peer = lax.rem(ctx + i, n_ctx)
            theirs = pl.ds(pl.multiple_of(peer * CHANS, CHANS), CHANS)
            pltpu.make_async_remote_copy(
                src_ref=source.at[theirs, :],
                dst_ref=target.at[mine, :],
                send_sem=swap_send.at[which],
                recv_sem=swap_recv.at[which],
                device_id={"ctx": peer},
                device_id_type=MESH,
            ).start()
            return carry

        lax.fori_loop(1, n_ctx, send, 0)
        target[mine, :] = source[mine, :]

    def exchanged(which, source, target):
        rows = pl.ds(0, (n_ctx - 1) * CHANS)
        return pltpu.make_async_remote_copy(
            src_ref=source.at[rows, :],
            dst_ref=target.at[rows, :],
            send_sem=swap_send.at[which],
            recv_sem=swap_recv.at[which],
            device_id={"ctx": lax.rem(ctx + 1, n_ctx)},
            device_id_type=MESH,
        )

    def token_blocks(buf):
        return [
            buf[pl.ds(j * CHANS, CHANS), :].astype(jnp.float32) for j in range(n_ctx)
        ]

    def put_blocks(buf, blocks):
        for j, block in enumerate(blocks):
            buf[pl.ds(j * CHANS, CHANS), :] = block.astype(jnp.bfloat16)

    for step in range(last):
        for turn in range(CHUNKS):
            for way in (0, 1):
                chunk = orders[way][turn]
                arrival(way, step, chunk).wait_recv()
                if way in ways(step + 1, chunk):
                    forward(way, step + 1, chunk)
            if step == 0 and turn == 1:
                pl.semaphore_wait(news, len(z_line))
                exchange(0, conv_buf, conv_in)
    for turn in range(CHUNKS // 2):
        for way in (0, 1):
            arrival(way, last, orders[way][turn]).wait_recv()

    loads[7].wait()
    loads[8].wait()
    tokens = ring[...].reshape(LANES, ring.shape[2])
    tile = min(128, unit.shape[0])

    def project(i, carry):
        rows = pl.ds(pl.multiple_of(i * tile, tile), tile)
        grad = lax.dot_general(
            weight[rows, :], tokens, (((1,), (1,)), ((), ())),
            preferred_element_type=jnp.float32,
        )
        unit[rows, :] = grad
        gate_send[rows, :] = (grad * gate_buf[rows, :].astype(jnp.float32)).astype(jnp.bfloat16)
        return carry

    lax.fori_loop(0, unit.shape[0] // tile, project, 0)
    exchange(1, gate_send, gate_in)

    exchanged(0, conv_buf, conv_in).wait_recv()
    ahead_transform(token_blocks(conv_in), twist, ahead, high, low, spec_conv)
    loads[5].wait()
    loads[6].wait()
    put_blocks(out_send, back_transform(
        lambda k: times(cell(spec_filt, k), cell(spec_conv, k)),
        n_ctx, untwist, back, high, low, spec_tmp,
    ))
    exchange(2, out_send, out_in)

    exchanged(1, gate_send, gate_in).wait_recv()
    ahead_transform(token_blocks(gate_in), twist, ahead, high, low, spec_gate)
    put_blocks(grad_send, back_transform(
        lambda k: times_conj(cell(spec_gate, k), cell(spec_filt, k)),
        n_ctx, untwist, back, high, low, spec_tmp,
    ))
    exchange(3, grad_send, grad_in)

    per = CHANS // n_dp
    group = n_dp
    filt_grads = back_transform(
        lambda k: times_conj(cell(spec_gate, k), cell(spec_conv, k)),
        n_ctx, untwist, back, high, low, spec_tmp,
    )
    for piece in range(n_dp):
        for j, block in enumerate(filt_grads):
            part_own[piece, j // group, pl.ds(j % group * per, per), :] = block[
                piece * per : (piece + 1) * per, :
            ]
    part_send[...] = part_own[...].astype(jnp.bfloat16)

    def part(i):
        peer = lax.rem(dp + i, n_dp)
        return pltpu.make_async_remote_copy(
            src_ref=part_send.at[peer],
            dst_ref=part_in.at[i - 1],
            send_sem=part_send_sem.at[i - 1],
            recv_sem=part_recv_sem.at[i - 1],
            device_id={"dp": peer},
            device_id_type=MESH,
        )

    parts = [part(i) for i in range(1, n_dp)]
    for copy in parts:
        copy.start()

    exchanged(2, out_send, out_in).wait_recv()
    gate_out[...] = (unit[...] * out_in[...].astype(jnp.float32)).astype(jnp.bfloat16)

    for copy in parts:
        copy.wait_recv()
    total = part_own[dp]
    for i in range(n_dp - 1):
        total = total + part_in[i].astype(jnp.float32)
    for j in range(n_ctx):
        filt_grad_out[:, pl.ds(j * LANES, LANES)] = total[
            j // group, j % group * per : (j % group + 1) * per, :
        ]

    exchanged(3, grad_send, grad_in).wait_recv()
    conv_grad_out[...] = grad_in[...]

    for copy in sends:
        copy.wait_send()
    for which, source, target in (
        (0, conv_buf, conv_in), (1, gate_send, gate_in),
        (2, out_send, out_in), (3, grad_send, grad_in),
    ):
        exchanged(which, source, target).wait_send()
    for copy in parts:
        copy.wait_send()


def hand_over(*refs):
    half = len(refs) // 2
    copies = [
        pltpu.make_async_copy(refs[i], refs[half + i], refs[-1].at[i]) for i in range(half)
    ]
    for copy in copies:
        copy.start()
    for copy in copies:
        copy.wait()


def on_device(sizes, out_grad, gate_in, conv_in, filter_raw, out_weight):
    n_ctx, n_tp, n_dp = sizes
    bf16, f32 = jnp.bfloat16, jnp.float32
    length = filter_raw.shape[1]
    depth = out_weight.shape[1]
    local = gate_in.shape[1]
    scale = 1.0 / math.sqrt(length) / (2 * length)
    twist, untwist, ahead, back = tables(n_ctx, scale)
    rows = (n_ctx + 1) * CHANS
    per = CHANS // n_dp
    vmem = pltpu.VMEM
    dma = pltpu.SemaphoreType.DMA
    whole = pl.BlockSpec(memory_space=pltpu.VMEM)
    grad, gate, filt = pl.pallas_call(
        functools.partial(kernel, n_ctx, n_tp, n_dp),
        out_shape=(
            vmem((local, LANES), bf16),
            vmem((local, LANES), bf16),
            vmem((per, length), f32),
        ),
        in_specs=[pl.BlockSpec(memory_space=pltpu.HBM)] * 9,
        out_specs=(whole, whole, whole),
        scratch_shapes=[
            vmem((n_tp, 16, depth), bf16),
            vmem((local, LANES), bf16),
            vmem((local, LANES), bf16),
            vmem((CHANS, length), f32),
            vmem((local, depth), bf16),
            vmem(twist.shape, f32),
            vmem(untwist.shape, f32),
            vmem(ahead.shape, bf16),
            vmem(back.shape, bf16),
            vmem((local, LANES), f32),
            *[vmem((local, LANES), bf16)] * 7,
            vmem((rows, 2 * LANES), bf16),
            vmem((rows, 2 * LANES), bf16),
            *[vmem((rows, 2 * LANES), f32)] * 4,
            vmem((n_dp, n_ctx // n_dp, CHANS, LANES), f32),
            vmem((n_dp, n_ctx // n_dp, CHANS, LANES), bf16),
            vmem((n_dp - 1, n_ctx // n_dp, CHANS, LANES), bf16),
            dma((9,)),
            dma((2, n_tp // 2, CHUNKS)),
            dma((2, n_tp // 2, CHUNKS)),
            dma((4,)),
            dma((4,)),
            dma((n_dp - 1,)),
            dma((n_dp - 1,)),
            pltpu.SemaphoreType.REGULAR,
        ],
        compiler_params=pltpu.CompilerParams(
            collective_id=0, has_side_effects=True, vmem_limit_bytes=MAIN_VMEM
        ),
    )(
        out_grad[0], gate_in[0], conv_in[0], filter_raw, out_weight,
        jnp.asarray(twist), jnp.asarray(untwist), jnp.asarray(ahead), jnp.asarray(back),
    )
    grad, gate, filt = pl.pallas_call(
        hand_over,
        out_shape=tuple(jax.ShapeDtypeStruct(a.shape, a.dtype) for a in (grad, gate, filt)),
        in_specs=[whole] * 3,
        out_specs=(pl.BlockSpec(memory_space=pltpu.HBM),) * 3,
        scratch_shapes=[dma((3,))],
        compiler_params=pltpu.CompilerParams(vmem_limit_bytes=FINISH_VMEM),
    )(grad, gate, filt)
    return grad[None], gate[None], filt


def solution(mesh):
    sizes = (mesh.shape["ctx"], mesh.shape["tp"], mesh.shape["dp"])
    placed = (
        P("dp", ("ctx", "tp"), None),
        P("dp", "tp", "ctx"),
        P("dp", "tp", "ctx"),
        P(("tp", "ctx"), None),
        P("tp", None),
    )
    return jax.shard_map(
        functools.partial(on_device, sizes),
        mesh=mesh,
        in_specs=placed,
        out_specs=(P("dp", "tp", "ctx"), P("dp", "tp", "ctx"), P(("tp", "ctx", "dp"), None)),
        check_vma=False,
    )
```

```python
import functools
import math

import jax
import jax.numpy as jnp
import numpy as np
from jax import lax
from jax.experimental import pallas as pl
from jax.experimental.pallas import tpu as pltpu
from jax.sharding import PartitionSpec as P

MESH = pl.DeviceIdType.MESH
LANES = 128
CHANS = 16
CHUNKS = 4
FINISH_VMEM = 1024 * 1024
MAIN_VMEM = 64000 * 1024


def wave(order, index):
    angle = 2.0 * math.pi * (index % order) / order
    return (math.cos(angle), math.sin(angle))


def plus(left, right):
    if left is None:
        return right
    if right is None:
        return left
    return left + right


def minus(left, right):
    if right is None:
        return left
    if left is None:
        return -right
    return left - right


def padded_spectrum(blocks):
    m = len(blocks)
    if m == 1:
        return [(blocks[0], None), (blocks[0], None)]
    even = padded_spectrum(blocks[0::2])
    odd = padded_spectrum(blocks[1::2])
    rows = [None] * (m + 1)
    rows[0] = (even[0][0] + odd[0][0], None)
    rows[m] = (even[0][0] - odd[0][0], None)
    for k in range(1, m // 2):
        cos, sin = wave(2 * m, k)
        odd_re, odd_im = odd[k]
        turn_re = odd_re * cos + odd_im * sin
        turn_im = odd_im * cos - odd_re * sin
        rows[k] = (even[k][0] + turn_re, even[k][1] + turn_im)
        rows[m - k] = (even[k][0] - turn_re, turn_im - even[k][1])
    rows[m // 2] = (even[m // 2][0], -odd[m // 2][0])
    return rows


def half_signal(rows):
    m = len(rows) - 1
    if m == 1:
        return [rows[0][0] + rows[1][0]]
    even, odd = [None] * (m // 2 + 1), [None] * (m // 2 + 1)
    even[0] = (rows[0][0] + rows[m][0], None)
    odd[0] = (rows[0][0] - rows[m][0], None)
    for k in range(1, m // 2):
        cos, sin = wave(2 * m, k)
        (low_re, low_im), (top_re, top_im) = rows[k], rows[m - k]
        even[k] = (low_re + top_re, low_im - top_im)
        diff_re, diff_im = low_re - top_re, low_im + top_im
        odd[k] = (diff_re * cos - diff_im * sin, diff_im * cos + diff_re * sin)
    even[m // 2] = (2.0 * rows[m // 2][0], None)
    odd[m // 2] = (-2.0 * rows[m // 2][1], None)
    blocks = [None] * m
    blocks[0::2] = half_signal(even)
    blocks[1::2] = half_signal(odd)
    return blocks


def in_two(table):
    high = table.astype(jnp.bfloat16)
    low = (table - np.asarray(high).astype(np.float64)).astype(jnp.bfloat16)
    return np.stack([np.asarray(high), np.asarray(low)])


def tables(blocks, scale):
    total = 2 * blocks * LANES
    rows = np.arange(blocks + 1)[:, None]
    lanes = np.arange(LANES)[None, :]
    angle = 2.0 * np.pi * (rows * lanes % total) / total
    twist = np.stack([np.cos(angle), -np.sin(angle)]).astype(np.float32)
    untwist = (np.stack([np.cos(angle), np.sin(angle)]) * scale).astype(np.float32)
    turn = 2.0 * np.pi * (lanes.T * lanes % LANES) / LANES
    cos, sin = np.cos(turn), np.sin(turn)
    ahead = in_two(np.block([[cos, -sin], [sin, cos]]))
    back = in_two(np.block([[cos, sin], [-sin, cos]]))
    return twist, untwist, ahead, back


def split_store(high, low, row, part, value):
    top = value.astype(jnp.bfloat16)
    rows = pl.ds(row * CHANS, CHANS)
    cols = pl.ds(part * LANES, LANES)
    high[rows, cols] = top
    low[rows, cols] = (value - top.astype(jnp.float32)).astype(jnp.bfloat16)


def inner(high, low, matrix, out):
    dot = functools.partial(jnp.dot, preferred_element_type=jnp.float32)
    out[...] = (
        dot(high[...], matrix[0]) + dot(low[...], matrix[0]) + dot(high[...], matrix[1])
    )


def cell(spectrum, row):
    rows = pl.ds(row * CHANS, CHANS)
    return spectrum[rows, pl.ds(0, LANES)], spectrum[rows, pl.ds(LANES, LANES)]


def ahead_transform(blocks, twist, matrix, high, low, out):
    for k, (re, im) in enumerate(padded_spectrum(blocks)):
        cos, sin = twist[0, pl.ds(k, 1), :], twist[1, pl.ds(k, 1), :]
        if im is None:
            split_store(high, low, k, 0, re * cos)
            split_store(high, low, k, 1, re * sin)
        else:
            split_store(high, low, k, 0, re * cos - im * sin)
            split_store(high, low, k, 1, re * sin + im * cos)
    inner(high, low, matrix, out)


def back_transform(product, count, untwist, matrix, high, low, out):
    for k in range(count + 1):
        re, im = product(k)
        split_store(high, low, k, 0, re)
        split_store(high, low, k, 1, im)
    inner(high, low, matrix, out)
    rows = []
    for k in range(count + 1):
        cos, sin = untwist[0, pl.ds(k, 1), :], untwist[1, pl.ds(k, 1), :]
        re, im = cell(out, k)
        real = re * cos - im * sin
        rows.append((real, None if k in (0, count) else re * sin + im * cos))
    return half_signal(rows)


def times(left, right):
    return (left[0] * right[0] - left[1] * right[1], left[0] * right[1] + left[1] * right[0])


def times_conj(left, right):
    return (left[0] * right[0] + left[1] * right[1], left[1] * right[0] - left[0] * right[1])


def kernel(
    n_ctx, n_tp, n_dp,
    grad_hbm, gate_hbm, conv_hbm, filt_hbm, weight_hbm,
    twist_hbm, untwist_hbm, ahead_hbm, back_hbm,
    gate_out, conv_grad_out, filt_grad_out,
    ring, gate_buf, conv_buf, filt_buf, weight, twist, untwist, ahead, back,
    unit, gate_send, out_send, grad_send, conv_in, gate_in, out_in, grad_in,
    high, low, spec_filt, spec_conv, spec_gate, spec_tmp, part_own, part_send, part_in,
    load_sem, ring_send, ring_recv, swap_send, swap_recv, part_send_sem, part_recv_sem,
    news,
):
    ctx, tp, dp = lax.axis_index("ctx"), lax.axis_index("tp"), lax.axis_index("dp")
    right, left = lax.rem(tp + 1, n_tp), lax.rem(tp + n_tp - 1, n_tp)

    n_y, n_z = n_ctx // 4, 2 * n_dp
    y, z, core = ctx // 4, lax.rem(ctx // 2, 2) * n_dp + dp, lax.rem(ctx, 2)

    def place(y_at, z_at, core_at):
        return {"ctx": y_at * 4 + z_at // n_dp * 2 + core_at, "dp": lax.rem(z_at, n_dp)}

    z_line = [place(y, lax.rem(z + d, n_z), core) for d in range(1, n_z)]
    y_lines = [
        place(lax.rem(y + d, n_y), z, lax.rem(core + c, 2))
        for d in range(n_y) for c in (0, 1) if d or c
    ]

    barrier = pltpu.get_barrier_semaphore()
    first = y_lines + z_line + [{"tp": right}, {"tp": left}]
    for peer in first:
        pl.semaphore_signal(barrier, inc=1, device_id=peer, device_id_type=MESH)

    loads = [
        pltpu.make_async_copy(src, dst, load_sem.at[i])
        for i, (src, dst) in enumerate(
            [
                (grad_hbm, ring.at[tp]), (conv_hbm, conv_buf), (filt_hbm, filt_buf),
                (twist_hbm, twist), (ahead_hbm, ahead), (untwist_hbm, untwist),
                (back_hbm, back), (weight_hbm, weight), (gate_hbm, gate_buf),
            ]
        )
    ]
    for load in loads:
        load.start()
    loads[0].wait()
    pl.semaphore_wait(barrier, len(first))

    width = ring.shape[2] // CHUNKS
    last = n_tp // 2 - 1

    def hop(way, step, chunk):
        origin = lax.rem(tp + step, n_tp) if way else lax.rem(tp + n_tp - step, n_tp)
        cols = pl.ds(chunk * width, width)
        block = ring.at[origin, :, cols]
        return pltpu.make_async_remote_copy(
            src_ref=block,
            dst_ref=block,
            send_sem=ring_send.at[way, step, chunk],
            recv_sem=ring_recv.at[way, step, chunk],
            device_id={"tp": left if way else right},
            device_id_type=MESH,
        )

    def arrival(way, step, chunk):
        origin = lax.rem(tp + step + 1, n_tp) if way else lax.rem(tp + n_tp - step - 1, n_tp)
        block = ring.at[origin, :, pl.ds(chunk * width, width)]
        return pltpu.make_async_remote_copy(
            src_ref=block,
            dst_ref=block,
            send_sem=ring_send.at[way, step, chunk],
            recv_sem=ring_recv.at[way, step, chunk],
            device_id={"tp": left if way else right},
            device_id_type=MESH,
        )

    def ways(step, chunk):
        if step < last:
            return (0, 1)
        return (0,) if chunk < CHUNKS // 2 else (1,)

    orders = (range(CHUNKS), [(c + CHUNKS // 2) % CHUNKS for c in range(CHUNKS)])
    sends = []

    def forward(way, step, chunk):
        copy = hop(way, step, chunk)
        copy.start()
        sends.append(copy)

    for turn in range(CHUNKS):
        for way in (0, 1):
            forward(way, 0, orders[way][turn])
    for peer in z_line:
        pl.semaphore_signal(news, inc=1, device_id=peer, device_id_type=MESH)

    loads[2].wait()
    loads[3].wait()
    loads[4].wait()
    ahead_transform(
        [filt_buf[:, pl.ds(j * LANES, LANES)] for j in range(n_ctx)],
        twist, ahead, high, low, spec_filt,
    )
    loads[1].wait()

    mine = pl.ds(pl.multiple_of(ctx * CHANS, CHANS), CHANS)

    def give(which, source, target, peer):
        theirs = pl.ds(pl.multiple_of(peer * CHANS, CHANS), CHANS)
        pltpu.make_async_remote_copy(
            src_ref=source.at[theirs, :],
            dst_ref=target.at[mine, :],
            send_sem=swap_send.at[which],
            recv_sem=swap_recv.at[which],
            device_id={"ctx": peer},
            device_id_type=MESH,
        ).start()

    y_at, side = ctx // 4, lax.rem(ctx, 4)

    def exchange(which, source, target):
        def send(a, carry):
            ahead_by = n_y // 2 + (a + 1) // 2 * (1 - 2 * lax.rem(a, 2))
            line = lax.rem(y_at + ahead_by, n_y) * 4
            for turn in (2, 3, 1, 0):
                give(which, source, target, line + lax.rem(side + turn, 4))
            return carry

        lax.fori_loop(0, n_y - 1, send, 0)
        for turn in (2, 3, 1):
            give(which, source, target, y_at * 4 + lax.rem(side + turn, 4))
        target[mine, :] = source[mine, :]

    def exchanged(which, source, target):
        rows = pl.ds(0, (n_ctx - 1) * CHANS)
        return pltpu.make_async_remote_copy(
            src_ref=source.at[rows, :],
            dst_ref=target.at[rows, :],
            send_sem=swap_send.at[which],
            recv_sem=swap_recv.at[which],
            device_id={"ctx": lax.rem(ctx + 1, n_ctx)},
            device_id_type=MESH,
        )

    def token_blocks(buf):
        return [
            buf[pl.ds(j * CHANS, CHANS), :].astype(jnp.float32) for j in range(n_ctx)
        ]

    def put_blocks(buf, blocks):
        for j, block in enumerate(blocks):
            buf[pl.ds(j * CHANS, CHANS), :] = block.astype(jnp.bfloat16)

    for step in range(last):
        for turn in range(CHUNKS):
            for way in (0, 1):
                chunk = orders[way][turn]
                arrival(way, step, chunk).wait_recv()
                if way in ways(step + 1, chunk):
                    forward(way, step + 1, chunk)
            if step == 0 and turn == 1:
                pl.semaphore_wait(news, len(z_line))
                exchange(0, conv_buf, conv_in)
    for turn in range(CHUNKS // 2):
        for way in (0, 1):
            arrival(way, last, orders[way][turn]).wait_recv()

    loads[7].wait()
    loads[8].wait()
    tokens = ring[...].reshape(LANES, ring.shape[2])
    per_tile = 8
    tile_rows = per_tile * CHANS
    n_tiles = n_ctx // per_tile
    my_tile, my_place = ctx // per_tile, lax.rem(ctx, per_tile)
    for k in sorted(range(n_tiles), key=lambda k: -min(k, n_tiles - k)):
        tile = lax.rem(my_tile + k, n_tiles)
        rows = pl.ds(pl.multiple_of(tile * tile_rows, tile_rows), tile_rows)
        grad = lax.dot_general(
            weight[rows, :], tokens, (((1,), (1,)), ((), ())),
            preferred_element_type=jnp.float32,
        )
        unit[rows, :] = grad
        gate_send[rows, :] = (grad * gate_buf[rows, :].astype(jnp.float32)).astype(jnp.bfloat16)

        def send_tile(r, carry, tile=tile, k=k):
            place_at = r if k else lax.rem(my_place + r, per_tile)
            give(1, gate_send, gate_in, tile * per_tile + place_at)
            return carry

        lax.fori_loop(0 if k else 1, per_tile, send_tile, 0)
    gate_in[mine, :] = gate_send[mine, :]

    exchanged(0, conv_buf, conv_in).wait_recv()
    ahead_transform(token_blocks(conv_in), twist, ahead, high, low, spec_conv)
    loads[5].wait()
    loads[6].wait()
    put_blocks(out_send, back_transform(
        lambda k: times(cell(spec_filt, k), cell(spec_conv, k)),
        n_ctx, untwist, back, high, low, spec_tmp,
    ))
    exchange(2, out_send, out_in)

    exchanged(1, gate_send, gate_in).wait_recv()
    ahead_transform(token_blocks(gate_in), twist, ahead, high, low, spec_gate)
    put_blocks(grad_send, back_transform(
        lambda k: times_conj(cell(spec_gate, k), cell(spec_filt, k)),
        n_ctx, untwist, back, high, low, spec_tmp,
    ))
    exchange(3, grad_send, grad_in)

    per = CHANS // n_dp
    group = n_dp
    filt_grads = back_transform(
        lambda k: times_conj(cell(spec_gate, k), cell(spec_conv, k)),
        n_ctx, untwist, back, high, low, spec_tmp,
    )
    for piece in range(n_dp):
        for j, block in enumerate(filt_grads):
            part_own[piece, j // group, pl.ds(j % group * per, per), :] = block[
                piece * per : (piece + 1) * per, :
            ]
    part_send[...] = part_own[...].astype(jnp.bfloat16)

    def part(i):
        peer = lax.rem(dp + i, n_dp)
        return pltpu.make_async_remote_copy(
            src_ref=part_send.at[peer],
            dst_ref=part_in.at[i - 1],
            send_sem=part_send_sem.at[i - 1],
            recv_sem=part_recv_sem.at[i - 1],
            device_id={"dp": peer},
            device_id_type=MESH,
        )

    parts = [part(i) for i in range(1, n_dp)]
    for copy in parts:
        copy.start()

    exchanged(2, out_send, out_in).wait_recv()
    gate_out[...] = (unit[...] * out_in[...].astype(jnp.float32)).astype(jnp.bfloat16)

    for copy in parts:
        copy.wait_recv()
    total = part_own[dp]
    for i in range(n_dp - 1):
        total = total + part_in[i].astype(jnp.float32)
    for j in range(n_ctx):
        filt_grad_out[:, pl.ds(j * LANES, LANES)] = total[
            j // group, j % group * per : (j % group + 1) * per, :
        ]

    exchanged(3, grad_send, grad_in).wait_recv()
    conv_grad_out[...] = grad_in[...]

    for copy in sends:
        copy.wait_send()
    for which, source, target in (
        (0, conv_buf, conv_in), (1, gate_send, gate_in),
        (2, out_send, out_in), (3, grad_send, grad_in),
    ):
        exchanged(which, source, target).wait_send()
    for copy in parts:
        copy.wait_send()


def hand_over(*refs):
    half = len(refs) // 2
    copies = [
        pltpu.make_async_copy(refs[i], refs[half + i], refs[-1].at[i]) for i in range(half)
    ]
    for copy in copies:
        copy.start()
    for copy in copies:
        copy.wait()


def on_device(sizes, out_grad, gate_in, conv_in, filter_raw, out_weight):
    n_ctx, n_tp, n_dp = sizes
    bf16, f32 = jnp.bfloat16, jnp.float32
    length = filter_raw.shape[1]
    depth = out_weight.shape[1]
    local = gate_in.shape[1]
    scale = 1.0 / math.sqrt(length) / (2 * length)
    twist, untwist, ahead, back = tables(n_ctx, scale)
    rows = (n_ctx + 1) * CHANS
    per = CHANS // n_dp
    vmem = pltpu.VMEM
    dma = pltpu.SemaphoreType.DMA
    whole = pl.BlockSpec(memory_space=pltpu.VMEM)
    grad, gate, filt = pl.pallas_call(
        functools.partial(kernel, n_ctx, n_tp, n_dp),
        out_shape=(
            vmem((local, LANES), bf16),
            vmem((local, LANES), bf16),
            vmem((per, length), f32),
        ),
        in_specs=[pl.BlockSpec(memory_space=pltpu.HBM)] * 9,
        out_specs=(whole, whole, whole),
        scratch_shapes=[
            vmem((n_tp, 16, depth), bf16),
            vmem((local, LANES), bf16),
            vmem((local, LANES), bf16),
            vmem((CHANS, length), f32),
            vmem((local, depth), bf16),
            vmem(twist.shape, f32),
            vmem(untwist.shape, f32),
            vmem(ahead.shape, bf16),
            vmem(back.shape, bf16),
            vmem((local, LANES), f32),
            *[vmem((local, LANES), bf16)] * 7,
            vmem((rows, 2 * LANES), bf16),
            vmem((rows, 2 * LANES), bf16),
            *[vmem((rows, 2 * LANES), f32)] * 4,
            vmem((n_dp, n_ctx // n_dp, CHANS, LANES), f32),
            vmem((n_dp, n_ctx // n_dp, CHANS, LANES), bf16),
            vmem((n_dp - 1, n_ctx // n_dp, CHANS, LANES), bf16),
            dma((9,)),
            dma((2, n_tp // 2, CHUNKS)),
            dma((2, n_tp // 2, CHUNKS)),
            dma((4,)),
            dma((4,)),
            dma((n_dp - 1,)),
            dma((n_dp - 1,)),
            pltpu.SemaphoreType.REGULAR,
        ],
        compiler_params=pltpu.CompilerParams(
            collective_id=0, has_side_effects=True, vmem_limit_bytes=MAIN_VMEM
        ),
    )(
        out_grad[0], gate_in[0], conv_in[0], filter_raw, out_weight,
        jnp.asarray(twist), jnp.asarray(untwist), jnp.asarray(ahead), jnp.asarray(back),
    )
    grad, gate, filt = pl.pallas_call(
        hand_over,
        out_shape=tuple(jax.ShapeDtypeStruct(a.shape, a.dtype) for a in (grad, gate, filt)),
        in_specs=[whole] * 3,
        out_specs=(pl.BlockSpec(memory_space=pltpu.HBM),) * 3,
        scratch_shapes=[dma((3,))],
        compiler_params=pltpu.CompilerParams(vmem_limit_bytes=FINISH_VMEM),
    )(grad, gate, filt)
    return grad[None], gate[None], filt


def solution(mesh):
    sizes = (mesh.shape["ctx"], mesh.shape["tp"], mesh.shape["dp"])
    placed = (
        P("dp", ("ctx", "tp"), None),
        P("dp", "tp", "ctx"),
        P("dp", "tp", "ctx"),
        P(("tp", "ctx"), None),
        P("tp", None),
    )
    return jax.shard_map(
        functools.partial(on_device, sizes),
        mesh=mesh,
        in_specs=placed,
        out_specs=(P("dp", "tp", "ctx"), P("dp", "tp", "ctx"), P(("tp", "ctx", "dp"), None)),
        check_vma=False,
    )
```

```python
import functools
import math

import jax
import jax.numpy as jnp
import numpy as np
from jax import lax
from jax.experimental import pallas as pl
from jax.experimental.pallas import tpu as pltpu
from jax.sharding import PartitionSpec as P

MESH = pl.DeviceIdType.MESH
LANES = 128
CHANS = 16
CHUNKS = 4
HEARD_AT = [(0, 1), (1, 0), (1, 3), (2, 2)]
FINISH_VMEM = 1024 * 1024
MAIN_VMEM = 64000 * 1024


def wave(order, index):
    angle = 2.0 * math.pi * (index % order) / order
    return (math.cos(angle), math.sin(angle))


def plus(left, right):
    if left is None:
        return right
    if right is None:
        return left
    return left + right


def minus(left, right):
    if right is None:
        return left
    if left is None:
        return -right
    return left - right


def padded_spectrum(blocks):
    m = len(blocks)
    if m == 1:
        return [(blocks[0], None), (blocks[0], None)]
    even = padded_spectrum(blocks[0::2])
    odd = padded_spectrum(blocks[1::2])
    rows = [None] * (m + 1)
    rows[0] = (even[0][0] + odd[0][0], None)
    rows[m] = (even[0][0] - odd[0][0], None)
    for k in range(1, m // 2):
        cos, sin = wave(2 * m, k)
        odd_re, odd_im = odd[k]
        turn_re = odd_re * cos + odd_im * sin
        turn_im = odd_im * cos - odd_re * sin
        rows[k] = (even[k][0] + turn_re, even[k][1] + turn_im)
        rows[m - k] = (even[k][0] - turn_re, turn_im - even[k][1])
    rows[m // 2] = (even[m // 2][0], -odd[m // 2][0])
    return rows


def half_signal(rows):
    m = len(rows) - 1
    if m == 1:
        return [rows[0][0] + rows[1][0]]
    even, odd = [None] * (m // 2 + 1), [None] * (m // 2 + 1)
    even[0] = (rows[0][0] + rows[m][0], None)
    odd[0] = (rows[0][0] - rows[m][0], None)
    for k in range(1, m // 2):
        cos, sin = wave(2 * m, k)
        (low_re, low_im), (top_re, top_im) = rows[k], rows[m - k]
        even[k] = (low_re + top_re, low_im - top_im)
        diff_re, diff_im = low_re - top_re, low_im + top_im
        odd[k] = (diff_re * cos - diff_im * sin, diff_im * cos + diff_re * sin)
    even[m // 2] = (2.0 * rows[m // 2][0], None)
    odd[m // 2] = (-2.0 * rows[m // 2][1], None)
    blocks = [None] * m
    blocks[0::2] = half_signal(even)
    blocks[1::2] = half_signal(odd)
    return blocks


def in_two(table):
    high = table.astype(jnp.bfloat16)
    low = (table - np.asarray(high).astype(np.float64)).astype(jnp.bfloat16)
    return np.stack([np.asarray(high), np.asarray(low)])


def tables(blocks, scale):
    total = 2 * blocks * LANES
    rows = np.arange(blocks + 1)[:, None]
    lanes = np.arange(LANES)[None, :]
    angle = 2.0 * np.pi * (rows * lanes % total) / total
    twist = np.stack([np.cos(angle), -np.sin(angle)]).astype(np.float32)
    untwist = (np.stack([np.cos(angle), np.sin(angle)]) * scale).astype(np.float32)
    turn = 2.0 * np.pi * (lanes.T * lanes % LANES) / LANES
    cos, sin = np.cos(turn), np.sin(turn)
    ahead = in_two(np.block([[cos, -sin], [sin, cos]]))
    back = in_two(np.block([[cos, sin], [-sin, cos]]))
    return twist, untwist, ahead, back


def split_store(high, low, row, part, value):
    top = value.astype(jnp.bfloat16)
    rows = pl.ds(row * CHANS, CHANS)
    cols = pl.ds(part * LANES, LANES)
    high[rows, cols] = top
    low[rows, cols] = (value - top.astype(jnp.float32)).astype(jnp.bfloat16)


def inner(high, low, matrix, out):
    dot = functools.partial(jnp.dot, preferred_element_type=jnp.float32)
    out[...] = (
        dot(high[...], matrix[0]) + dot(low[...], matrix[0]) + dot(high[...], matrix[1])
    )


def cell(spectrum, row):
    rows = pl.ds(row * CHANS, CHANS)
    return spectrum[rows, pl.ds(0, LANES)], spectrum[rows, pl.ds(LANES, LANES)]


def ahead_transform(blocks, twist, matrix, high, low, out):
    for k, (re, im) in enumerate(padded_spectrum(blocks)):
        cos, sin = twist[0, pl.ds(k, 1), :], twist[1, pl.ds(k, 1), :]
        if im is None:
            split_store(high, low, k, 0, re * cos)
            split_store(high, low, k, 1, re * sin)
        else:
            split_store(high, low, k, 0, re * cos - im * sin)
            split_store(high, low, k, 1, re * sin + im * cos)
    inner(high, low, matrix, out)


def back_transform(product, count, untwist, matrix, high, low, out):
    for k in range(count + 1):
        re, im = product(k)
        split_store(high, low, k, 0, re)
        split_store(high, low, k, 1, im)
    inner(high, low, matrix, out)
    rows = []
    for k in range(count + 1):
        cos, sin = untwist[0, pl.ds(k, 1), :], untwist[1, pl.ds(k, 1), :]
        re, im = cell(out, k)
        real = re * cos - im * sin
        rows.append((real, None if k in (0, count) else re * sin + im * cos))
    return half_signal(rows)


def times(left, right):
    return (left[0] * right[0] - left[1] * right[1], left[0] * right[1] + left[1] * right[0])


def times_conj(left, right):
    return (left[0] * right[0] + left[1] * right[1], left[1] * right[0] - left[0] * right[1])


def kernel(
    n_ctx, n_tp, n_dp,
    grad_hbm, gate_hbm, conv_hbm, filt_hbm, weight_hbm,
    twist_hbm, untwist_hbm, ahead_hbm, back_hbm,
    gate_out, conv_grad_out, filt_grad_out,
    ring, gate_buf, conv_buf, filt_buf, weight, twist, untwist, ahead, back,
    unit, gate_send, out_send, grad_send, conv_in, gate_in, out_in, grad_in,
    high, low, spec_filt, spec_conv, spec_gate, spec_tmp, part_own, part_send, part_in,
    load_sem, ring_send, ring_recv, swap_send, swap_recv, part_send_sem, part_recv_sem,
    news,
):
    ctx, tp, dp = lax.axis_index("ctx"), lax.axis_index("tp"), lax.axis_index("dp")
    right, left = lax.rem(tp + 1, n_tp), lax.rem(tp + n_tp - 1, n_tp)

    n_y, n_z = n_ctx // 4, 2 * n_dp
    y, z, core = ctx // 4, lax.rem(ctx // 2, 2) * n_dp + dp, lax.rem(ctx, 2)

    def place(y_at, z_at, core_at):
        return {"ctx": y_at * 4 + z_at // n_dp * 2 + core_at, "dp": lax.rem(z_at, n_dp)}

    def offsets(size, *steps):
        return sorted({d % size for step in steps for d in (step, -step)} - {0})

    y_two = [place(lax.rem(y + d, n_y), z, core) for d in offsets(n_y, 2)]
    z_two = [place(y, lax.rem(z + d, n_z), core) for d in offsets(n_z, 2)]
    y_near = [place(lax.rem(y + d, n_y), z, core) for d in offsets(n_y, 1, 2)]
    z_near = [place(y, lax.rem(z + d, n_z), core) for d in offsets(n_z, 1, 2)]
    other_core = [place(y, z, 1 - core)]

    barrier = pltpu.get_barrier_semaphore()
    first = y_near + z_near + other_core + [{"tp": right}, {"tp": left}]
    for peer in first:
        pl.semaphore_signal(barrier, inc=1, device_id=peer, device_id_type=MESH)
    rounds = [z_near]
    if n_y > 4:
        rounds.insert(0, y_two)
    if n_z > 4:
        rounds.append(z_two)
    rounds.append(other_core)

    def tell(at):
        for peer in rounds[at]:
            pl.semaphore_signal(news.at[at], inc=1, device_id=peer, device_id_type=MESH)

    def hear(at):
        pl.semaphore_wait(news.at[at], len(rounds[at]))
        if at + 1 < len(rounds):
            tell(at + 1)

    loads = [
        pltpu.make_async_copy(src, dst, load_sem.at[i])
        for i, (src, dst) in enumerate(
            [
                (grad_hbm, ring.at[tp]), (conv_hbm, conv_buf), (filt_hbm, filt_buf),
                (twist_hbm, twist), (ahead_hbm, ahead), (untwist_hbm, untwist),
                (back_hbm, back), (weight_hbm, weight), (gate_hbm, gate_buf),
            ]
        )
    ]
    for load in loads:
        load.start()
    loads[0].wait()
    pl.semaphore_wait(barrier, len(first))

    width = ring.shape[2] // CHUNKS
    last = n_tp // 2 - 1

    def hop(way, step, chunk):
        origin = lax.rem(tp + step, n_tp) if way else lax.rem(tp + n_tp - step, n_tp)
        cols = pl.ds(chunk * width, width)
        block = ring.at[origin, :, cols]
        return pltpu.make_async_remote_copy(
            src_ref=block,
            dst_ref=block,
            send_sem=ring_send.at[way, step, chunk],
            recv_sem=ring_recv.at[way, step, chunk],
            device_id={"tp": left if way else right},
            device_id_type=MESH,
        )

    def arrival(way, step, chunk):
        origin = lax.rem(tp + step + 1, n_tp) if way else lax.rem(tp + n_tp - step - 1, n_tp)
        block = ring.at[origin, :, pl.ds(chunk * width, width)]
        return pltpu.make_async_remote_copy(
            src_ref=block,
            dst_ref=block,
            send_sem=ring_send.at[way, step, chunk],
            recv_sem=ring_recv.at[way, step, chunk],
            device_id={"tp": left if way else right},
            device_id_type=MESH,
        )

    def ways(step, chunk):
        if step < last:
            return (0, 1)
        return (0,) if chunk < CHUNKS // 2 else (1,)

    orders = (range(CHUNKS), [(c + CHUNKS // 2) % CHUNKS for c in range(CHUNKS)])
    sends = []

    def forward(way, step, chunk):
        copy = hop(way, step, chunk)
        copy.start()
        sends.append(copy)

    for turn in range(CHUNKS):
        for way in (0, 1):
            forward(way, 0, orders[way][turn])
    tell(0)

    loads[2].wait()
    loads[3].wait()
    loads[4].wait()
    ahead_transform(
        [filt_buf[:, pl.ds(j * LANES, LANES)] for j in range(n_ctx)],
        twist, ahead, high, low, spec_filt,
    )
    loads[1].wait()

    mine = pl.ds(pl.multiple_of(ctx * CHANS, CHANS), CHANS)

    def give(which, source, target, peer):
        theirs = pl.ds(pl.multiple_of(peer * CHANS, CHANS), CHANS)
        pltpu.make_async_remote_copy(
            src_ref=source.at[theirs, :],
            dst_ref=target.at[mine, :],
            send_sem=swap_send.at[which],
            recv_sem=swap_recv.at[which],
            device_id={"ctx": peer},
            device_id_type=MESH,
        ).start()

    y_at, side = ctx // 4, lax.rem(ctx, 4)

    def exchange(which, source, target):
        def send(a, carry):
            ahead_by = n_y // 2 + (a + 1) // 2 * (1 - 2 * lax.rem(a, 2))
            line = lax.rem(y_at + ahead_by, n_y) * 4
            for turn in (2, 3, 1, 0):
                give(which, source, target, line + lax.rem(side + turn, 4))
            return carry

        lax.fori_loop(0, n_y - 1, send, 0)
        for turn in (2, 3, 1):
            give(which, source, target, y_at * 4 + lax.rem(side + turn, 4))
        target[mine, :] = source[mine, :]

    def exchanged(which, source, target):
        rows = pl.ds(0, (n_ctx - 1) * CHANS)
        return pltpu.make_async_remote_copy(
            src_ref=source.at[rows, :],
            dst_ref=target.at[rows, :],
            send_sem=swap_send.at[which],
            recv_sem=swap_recv.at[which],
            device_id={"ctx": lax.rem(ctx + 1, n_ctx)},
            device_id_type=MESH,
        )

    def token_blocks(buf):
        return [
            buf[pl.ds(j * CHANS, CHANS), :].astype(jnp.float32) for j in range(n_ctx)
        ]

    def put_blocks(buf, blocks):
        for j, block in enumerate(blocks):
            buf[pl.ds(j * CHANS, CHANS), :] = block.astype(jnp.bfloat16)

    for step in range(last):
        for turn in range(CHUNKS):
            for way in (0, 1):
                chunk = orders[way][turn]
                arrival(way, step, chunk).wait_recv()
                if way in ways(step + 1, chunk):
                    forward(way, step + 1, chunk)
            if (step, turn) in HEARD_AT[: len(rounds)]:
                at = HEARD_AT.index((step, turn))
                hear(at)
                if at + 1 == len(rounds):
                    exchange(0, conv_buf, conv_in)
    for turn in range(CHUNKS // 2):
        for way in (0, 1):
            arrival(way, last, orders[way][turn]).wait_recv()

    loads[7].wait()
    loads[8].wait()
    tokens = ring[...].reshape(LANES, ring.shape[2])
    per_tile = 8
    tile_rows = per_tile * CHANS
    n_tiles = n_ctx // per_tile
    my_tile, my_place = ctx // per_tile, lax.rem(ctx, per_tile)
    for k in sorted(range(n_tiles), key=lambda k: -min(k, n_tiles - k)):
        tile = lax.rem(my_tile + k, n_tiles)
        rows = pl.ds(pl.multiple_of(tile * tile_rows, tile_rows), tile_rows)
        grad = lax.dot_general(
            weight[rows, :], tokens, (((1,), (1,)), ((), ())),
            preferred_element_type=jnp.float32,
        )
        unit[rows, :] = grad
        gate_send[rows, :] = (grad * gate_buf[rows, :].astype(jnp.float32)).astype(jnp.bfloat16)

        def send_tile(r, carry, tile=tile, k=k):
            place_at = r if k else lax.rem(my_place + r, per_tile)
            give(1, gate_send, gate_in, tile * per_tile + place_at)
            return carry

        lax.fori_loop(0 if k else 1, per_tile, send_tile, 0)
    gate_in[mine, :] = gate_send[mine, :]

    exchanged(0, conv_buf, conv_in).wait_recv()
    ahead_transform(token_blocks(conv_in), twist, ahead, high, low, spec_conv)
    loads[5].wait()
    loads[6].wait()
    put_blocks(out_send, back_transform(
        lambda k: times(cell(spec_filt, k), cell(spec_conv, k)),
        n_ctx, untwist, back, high, low, spec_tmp,
    ))
    exchange(2, out_send, out_in)

    exchanged(1, gate_send, gate_in).wait_recv()
    ahead_transform(token_blocks(gate_in), twist, ahead, high, low, spec_gate)
    put_blocks(grad_send, back_transform(
        lambda k: times_conj(cell(spec_gate, k), cell(spec_filt, k)),
        n_ctx, untwist, back, high, low, spec_tmp,
    ))
    exchange(3, grad_send, grad_in)

    per = CHANS // n_dp
    group = n_dp
    filt_grads = back_transform(
        lambda k: times_conj(cell(spec_gate, k), cell(spec_conv, k)),
        n_ctx, untwist, back, high, low, spec_tmp,
    )
    for piece in range(n_dp):
        for j, block in enumerate(filt_grads):
            part_own[piece, j // group, pl.ds(j % group * per, per), :] = block[
                piece * per : (piece + 1) * per, :
            ]
    part_send[...] = part_own[...].astype(jnp.bfloat16)

    def part(i):
        peer = lax.rem(dp + i, n_dp)
        return pltpu.make_async_remote_copy(
            src_ref=part_send.at[peer],
            dst_ref=part_in.at[i - 1],
            send_sem=part_send_sem.at[i - 1],
            recv_sem=part_recv_sem.at[i - 1],
            device_id={"dp": peer},
            device_id_type=MESH,
        )

    parts = [part(i) for i in range(1, n_dp)]
    for copy in parts:
        copy.start()

    exchanged(2, out_send, out_in).wait_recv()
    gate_out[...] = (unit[...] * out_in[...].astype(jnp.float32)).astype(jnp.bfloat16)

    for copy in parts:
        copy.wait_recv()
    total = part_own[dp]
    for i in range(n_dp - 1):
        total = total + part_in[i].astype(jnp.float32)
    for j in range(n_ctx):
        filt_grad_out[:, pl.ds(j * LANES, LANES)] = total[
            j // group, j % group * per : (j % group + 1) * per, :
        ]

    exchanged(3, grad_send, grad_in).wait_recv()
    conv_grad_out[...] = grad_in[...]

    for copy in sends:
        copy.wait_send()
    for which, source, target in (
        (0, conv_buf, conv_in), (1, gate_send, gate_in),
        (2, out_send, out_in), (3, grad_send, grad_in),
    ):
        exchanged(which, source, target).wait_send()
    for copy in parts:
        copy.wait_send()


def hand_over(*refs):
    half = len(refs) // 2
    copies = [
        pltpu.make_async_copy(refs[i], refs[half + i], refs[-1].at[i]) for i in range(half)
    ]
    for copy in copies:
        copy.start()
    for copy in copies:
        copy.wait()


def on_device(sizes, out_grad, gate_in, conv_in, filter_raw, out_weight):
    n_ctx, n_tp, n_dp = sizes
    bf16, f32 = jnp.bfloat16, jnp.float32
    length = filter_raw.shape[1]
    depth = out_weight.shape[1]
    local = gate_in.shape[1]
    scale = 1.0 / math.sqrt(length) / (2 * length)
    twist, untwist, ahead, back = tables(n_ctx, scale)
    rows = (n_ctx + 1) * CHANS
    per = CHANS // n_dp
    vmem = pltpu.VMEM
    dma = pltpu.SemaphoreType.DMA
    whole = pl.BlockSpec(memory_space=pltpu.VMEM)
    grad, gate, filt = pl.pallas_call(
        functools.partial(kernel, n_ctx, n_tp, n_dp),
        out_shape=(
            vmem((local, LANES), bf16),
            vmem((local, LANES), bf16),
            vmem((per, length), f32),
        ),
        in_specs=[pl.BlockSpec(memory_space=pltpu.HBM)] * 9,
        out_specs=(whole, whole, whole),
        scratch_shapes=[
            vmem((n_tp, 16, depth), bf16),
            vmem((local, LANES), bf16),
            vmem((local, LANES), bf16),
            vmem((CHANS, length), f32),
            vmem((local, depth), bf16),
            vmem(twist.shape, f32),
            vmem(untwist.shape, f32),
            vmem(ahead.shape, bf16),
            vmem(back.shape, bf16),
            vmem((local, LANES), f32),
            *[vmem((local, LANES), bf16)] * 7,
            vmem((rows, 2 * LANES), bf16),
            vmem((rows, 2 * LANES), bf16),
            *[vmem((rows, 2 * LANES), f32)] * 4,
            vmem((n_dp, n_ctx // n_dp, CHANS, LANES), f32),
            vmem((n_dp, n_ctx // n_dp, CHANS, LANES), bf16),
            vmem((n_dp - 1, n_ctx // n_dp, CHANS, LANES), bf16),
            dma((9,)),
            dma((2, n_tp // 2, CHUNKS)),
            dma((2, n_tp // 2, CHUNKS)),
            dma((4,)),
            dma((4,)),
            dma((n_dp - 1,)),
            dma((n_dp - 1,)),
            pltpu.SemaphoreType.REGULAR((len(HEARD_AT),)),
        ],
        compiler_params=pltpu.CompilerParams(
            collective_id=0, has_side_effects=True, vmem_limit_bytes=MAIN_VMEM
        ),
    )(
        out_grad[0], gate_in[0], conv_in[0], filter_raw, out_weight,
        jnp.asarray(twist), jnp.asarray(untwist), jnp.asarray(ahead), jnp.asarray(back),
    )
    grad, gate, filt = pl.pallas_call(
        hand_over,
        out_shape=tuple(jax.ShapeDtypeStruct(a.shape, a.dtype) for a in (grad, gate, filt)),
        in_specs=[whole] * 3,
        out_specs=(pl.BlockSpec(memory_space=pltpu.HBM),) * 3,
        scratch_shapes=[dma((3,))],
        compiler_params=pltpu.CompilerParams(vmem_limit_bytes=FINISH_VMEM),
    )(grad, gate, filt)
    return grad[None], gate[None], filt


def solution(mesh):
    sizes = (mesh.shape["ctx"], mesh.shape["tp"], mesh.shape["dp"])
    placed = (
        P("dp", ("ctx", "tp"), None),
        P("dp", "tp", "ctx"),
        P("dp", "tp", "ctx"),
        P(("tp", "ctx"), None),
        P("tp", None),
    )
    return jax.shard_map(
        functools.partial(on_device, sizes),
        mesh=mesh,
        in_specs=placed,
        out_specs=(P("dp", "tp", "ctx"), P("dp", "tp", "ctx"), P(("tp", "ctx", "dp"), None)),
        check_vma=False,
    )
```
